512 devices in a mesh: band: 16 (over z_hi, x), grid: 32 (over z_lo, y, core).
Axes of the slice: x: 4, y: 8, z: 8 (z_hi: 4, z_lo: 2; z = z_hi * 2 + z_lo), core: 2. Of those that a mesh axis runs over, the one named last changes fastest.
Arguments:
- valence: bfloat16 [256, 96, 9216], P('band', 'grid'), may hold values from -6 to 6
- conduction: bfloat16 [128, 96, 9216], P('band', 'grid'), may hold values from -6 to 6
- screened: bfloat16 [6144, 6144], P('grid'), may hold values from -0.0007324219 to 0.0007324219
- blocks: int32 [2], replicated, may hold values from 0 to 31
- gsphere: int32 [6144], P('grid'), may hold values from 0 to 1023, as said below
Outputs:
- kernel: float32 [16, 64, 64], P('band', 'grid')
The draws below stay inside these ranges and needn't reach their ends.
Inputs may be any that keep to these rules, and one draw needn't show every extreme that they name: `gsphere`: distinct within each aligned block of 192 entries.
All inputs are finite; a program needn't handle non-finite values.
Results may differ from the reference program's by a relative error of at most 0.0093.
Values may be sent and summed in bfloat16 or wider, within the bound.
A program may use at most 64 MiB of HBM per device.

```python
import math
import jax
import jax.numpy as jnp
from jax import lax

GRID_N = 96
KF = 32
NG = 6144
CB_DEV = 8
BLK = 8
CB = 128
NB = 32
NVAL = 256
NG_DEV = 192
N_BAND = 16
N_GRID = 32


def draw_gsphere(key, part):
    per_block = NG // N_GRID
    local_count = KF * KF * (KF // N_GRID)
    keys = jax.random.split(jax.random.fold_in(key, 17), N_GRID)

    def one_block(block_key):
        first_key, second_key = jax.random.split(block_key)
        inner = jax.random.permutation(first_key, local_count - 2)[:per_block - 2] + 1
        values = jnp.concatenate([jnp.array([0, local_count - 1], dtype=jnp.int32), inner.astype(jnp.int32)])
        return jax.random.permutation(second_key, values)
    return jax.vmap(one_block)(keys).reshape(NG).astype(jnp.int32)


def block_scale(own_key, shape, cuts, least, high):
    def one(axis_at, blocks):
        heights = jax.random.uniform(jax.random.fold_in(jax.random.fold_in(own_key, 6), axis_at), (blocks,), jnp.float32, least / len(cuts), high / len(cuts))
        return jnp.repeat(jnp.exp(heights), shape[axis_at] // blocks).reshape((-1,) + (1,) * (len(shape) - axis_at - 1))

    gain = one(*cuts[0])
    for cut in cuts[1:]:
        gain = gain * one(*cut)
    return gain


def gaussian(own_key, dims, scale, reach, pieces=(), held_as=jnp.bfloat16):
    factor_of = block_scale(own_key, dims, pieces, -0.22, 0.18) if pieces else 1.0
    values = jax.random.normal(own_key, dims, jnp.float32) * scale * factor_of
    return jnp.minimum(jnp.maximum(values, -reach), reach).astype(held_as)


def setup_inputs(seed: int = 0) -> dict:
    key_of = jax.random.split(jax.random.key(seed), 6)
    valence = gaussian(key_of[0], (NVAL, GRID_N, GRID_N * GRID_N), 1.0, 6.0, ((0, 16), (1, 32)))
    conduction = gaussian(key_of[1], (CB, GRID_N, GRID_N * GRID_N), 1.0, 6.0, ((0, 16), (1, 32)))
    screened = gaussian(key_of[2], (NG, NG), (2 * NG * NG) ** -0.5, 0.0007324219, ((0, 32),))
    blocks = jax.random.randint(key_of[3], (2,), 0, NB).astype(jnp.int32)
    gsphere = draw_gsphere(jax.random.fold_in(key_of[5], 71), 0)
    return {"valence": valence, "conduction": conduction, "screened": screened, "blocks": blocks, "gsphere": gsphere}


def fourier_parts(length, kept):
    positions = jnp.arange(length, dtype=jnp.int32)
    freqs = jnp.arange(kept, dtype=jnp.int32) - kept // 2
    phase = positions[:, None] * freqs[None, :] % length
    phases = phase.astype(jnp.float32) * (2.0 * math.pi / length)
    factor = 1.0 / math.sqrt(length)
    return (jnp.cos(phases) * factor, jnp.sin(phases) * factor)

def first_table(length, kept):
    cosine, sine = fourier_parts(length, kept)
    return jnp.stack([cosine, -sine], axis=2).astype(jnp.bfloat16)

def mixing_table(length, kept):
    cosine, sine = fourier_parts(length, kept)
    real_rows = jnp.stack([cosine, sine], axis=-1)
    imag_rows = jnp.stack([-sine, cosine], axis=-1)
    return jnp.stack([real_rows, imag_rows], axis=2).astype(jnp.bfloat16)

def reference(valence, conduction, screened, blocks, gsphere):
    z_table = first_table(GRID_N, KF).astype(jnp.float32)
    mixing = mixing_table(GRID_N, KF).astype(jnp.float32)
    high = lax.Precision.HIGHEST
    pick_a = lax.dynamic_slice_in_dim(valence, (blocks[0] * BLK).astype(jnp.int32), BLK, 0)
    pick_b = lax.dynamic_slice_in_dim(valence, (blocks[1] * BLK).astype(jnp.int32), BLK, 0)
    chosen = jnp.concatenate([pick_a, pick_b], axis=0)
    planes = KF // N_GRID
    number = jnp.arange(NG, dtype=jnp.int32)
    owner = number // NG_DEV
    freq_x = gsphere // (planes * KF)
    freq_y = owner * planes + gsphere // KF % planes
    freq_z = gsphere % KF
    index = ((freq_x * KF + freq_y) * KF + freq_z).astype(jnp.int32)
    cond_groups = conduction.reshape(N_BAND, CB_DEV, GRID_N, GRID_N * GRID_N)
    pairs = BLK * CB_DEV

    def per_band(cond):

        def per_valence(orbital):
            density = (orbital[None] * cond).reshape(CB_DEV, GRID_N, GRID_N, GRID_N)
            z_section = jnp.einsum('cxyz,zqi->cxyqi', density.astype(jnp.float32), z_table, precision=high).astype(jnp.bfloat16)
            y_section = jnp.einsum('cxyqi,ykoi->cxkqo', z_section.astype(jnp.float32), mixing, precision=high).astype(jnp.bfloat16)
            x_section = jnp.einsum('cxjqi,xkoi->ckjqo', y_section.astype(jnp.float32), mixing, precision=high).astype(jnp.bfloat16)
            flat = x_section.reshape(CB_DEV, KF * KF * KF, 2)
            return jnp.take(flat, index, axis=1)
        sphere = lax.map(per_valence, chosen)
        sphere = jnp.transpose(sphere, (2, 3, 0, 1)).reshape(NG, 2, 2 * pairs)
        side_a = sphere[:, :, :pairs]
        side_b = sphere[:, :, pairs:]
        screened_b = jnp.dot(screened, side_b.reshape(NG, 2 * pairs), preferred_element_type=jnp.float32)
        screened_b = screened_b.astype(jnp.bfloat16).reshape(NG, 2, pairs)
        return jnp.einsum('npi,npj->ij', side_a.astype(jnp.float32), screened_b.astype(jnp.float32), precision=high)
    return lax.map(per_band, cond_groups)
```

```python
import functools
import math

import jax
import jax.numpy as jnp
import ml_dtypes
import numpy as np
from jax import lax
from jax.experimental import pallas as pl
from jax.experimental.pallas import tpu as pltpu
from jax.sharding import PartitionSpec as P

GRID_N = 96
KF = 32
BLK = 8
PAIRS = 64
SIDE = 4
LANES = GRID_N * GRID_N
PART = LANES // 2
PIECE = PART // SIDE
ROWS_Y = 4
CHUNK = ROWS_Y * GRID_N
MESH = pl.DeviceIdType.MESH


def fourier_parts(length, kept):
    positions = np.arange(length)
    freqs = np.arange(kept) - kept // 2
    phases = (positions[:, None] * freqs[None, :] % length) * (2.0 * math.pi / length)
    factor = 1.0 / math.sqrt(length)
    return np.cos(phases) * factor, np.sin(phases) * factor


def first_table():
    cosine, sine = fourier_parts(GRID_N, KF)
    return np.stack([cosine, -sine], axis=2)


def mixing_table():
    cosine, sine = fourier_parts(GRID_N, KF)
    real_rows = np.stack([cosine, sine], axis=-1)
    imag_rows = np.stack([-sine, cosine], axis=-1)
    return np.stack([real_rows, imag_rows], axis=2)


def z_matrix():
    table = first_table()
    out = np.zeros((KF, ROWS_Y, 2, ROWS_Y, GRID_N))
    for y in range(ROWS_Y):
        out[:, y, :, y, :] = np.transpose(table, (1, 2, 0))
    return out.reshape(KF * ROWS_Y * 2, CHUNK).astype(ml_dtypes.bfloat16)


def mix_matrix():
    table = np.transpose(mixing_table(), (1, 2, 0, 3))
    return table.reshape(2 * KF, 2 * GRID_N).astype(ml_dtypes.bfloat16)


def remote(src, dst, send, recv, peer):
    return pltpu.make_async_remote_copy(
        src_ref=src, dst_ref=dst, send_sem=send, recv_sem=recv, device_id=peer, device_id_type=MESH
    )


def greet(peers):
    barrier = pltpu.get_barrier_semaphore()
    for peer in peers:
        pl.semaphore_signal(barrier, inc=1, device_id=peer, device_id_type=MESH)
    pl.semaphore_wait(barrier, len(peers))


def spread_kernel(
    owner_ref, src, out_ref, near0, near1, near2, near3, held, far, mine, full,
    send1, recv1, own1, send2, recv2, send3, recv3, send4, recv4,
):
    band = lax.axis_index("band")
    z, x = band // SIDE, band % SIDE
    near = (near0, near1, near2, near3)

    def along_x(k):
        return {"band": z * SIDE + (x + k) % SIDE}

    def along_z(k):
        return {"band": (z + k) % SIDE * SIDE + x}

    def lanes(q, s):
        return pl.ds(pl.multiple_of(q % 2 * PART + s * PIECE, 128), PIECE)

    greet([along_x(k) for k in (1, 2, 3)] + [along_z(k) for k in (1, 2, 3)])
    order = (2, 1, 3, 0)
    first = {}
    for j in order:
        s = (z + j) % SIDE
        for k in (2, 1, 3):
            q = (x + k) % SIDE
            copy = remote(
                src.at[q // 2, :, :, lanes(q, s)], near[j].at[x],
                send1.at[j, k - 1], recv1.at[j, k - 1], along_x(k),
            )
            copy.start()
            first[j, k] = copy
        copy = pltpu.make_async_copy(src.at[x // 2, :, :, lanes(x, s)], near[j].at[x], own1.at[j])
        copy.start()
        first[j, 0] = copy
    owner = owner_ref[x // 2]
    owner_z, owner_x = owner // SIDE, owner % SIDE
    second = []
    for j in order:
        for k in range(SIDE):
            first[j, k].wait()
        if j == 0:
            far[z] = near[j][owner_x]
        else:
            held[j] = near[j][owner_x]
            copy = remote(
                held.at[j], far.at[z], send2.at[j - 1], recv2.at[j - 1], along_z(j)
            )
            copy.start()
            second.append(copy)
    for copy in second:
        copy.wait()
    picked = far[owner_z]
    mine[...] = picked
    full[x // 2, :, :, lanes(x, z)] = picked
    third = {}
    for k in (2, 1, 3):
        copy = remote(
            mine, full.at[x // 2, :, :, lanes(x, z)], send3.at[k - 1], recv3.at[k - 1], along_z(k)
        )
        copy.start()
        third[k] = copy
    fourth = []
    for j in (0, 1, 3, 2):
        if j:
            third[j].wait()
        s = (z + SIDE - j) % SIDE
        part = full.at[x // 2, :, :, lanes(x, s)]
        for k in (2, 1, 3):
            copy = remote(
                mine if j == 0 else part, part, send4.at[j, k - 1], recv4.at[j, k - 1], along_x(k)
            )
            copy.start()
            fourth.append(copy)
    for copy in fourth:
        copy.wait()
    out_ref[...] = full[...]


def spread(owner, pieces):
    piece = (3, BLK, PIECE)
    dma = pltpu.SemaphoreType.DMA
    vmem = pl.BlockSpec(memory_space=pltpu.VMEM)
    return pl.pallas_call(
        spread_kernel,
        out_shape=jax.ShapeDtypeStruct(pieces.shape, pieces.dtype),
        in_specs=[pl.BlockSpec(memory_space=pltpu.SMEM), vmem],
        out_specs=vmem,
        scratch_shapes=[
            *[pltpu.VMEM((SIDE, *piece), jnp.bfloat16) for _ in range(SIDE)],
            pltpu.VMEM((SIDE, *piece), jnp.bfloat16),
            pltpu.VMEM((SIDE, *piece), jnp.bfloat16),
            pltpu.VMEM(piece, jnp.bfloat16),
            pltpu.VMEM(pieces.shape, jnp.bfloat16),
            dma((SIDE, 3)), dma((SIDE, 3)), dma((SIDE,)),
            dma((3,)), dma((3,)), dma((3,)), dma((3,)),
            dma((SIDE, 3)), dma((SIDE, 3)),
        ],
        compiler_params=pltpu.CompilerParams(collective_id=0, has_side_effects=True),
        name="spread_blocks",
    )(owner, pieces)


def density_kernel(chosen, cond, z_mat, mix, out_ref, sections):
    def step(j, carry):
        both = []
        for half in range(2):
            at = pl.ds(pl.multiple_of((2 * j + half) * CHUNK, 128), CHUNK)
            c = cond[0, :, at].astype(jnp.float32)
            v = jnp.concatenate(
                [chosen[0, 0, :, at].astype(jnp.float32), chosen[1, 0, :, at].astype(jnp.float32)]
            )
            dens = (v[:, None, :] * c[None, :, :]).reshape(2 * PAIRS, CHUNK).astype(jnp.bfloat16)
            part = lax.dot_general(
                z_mat[...], dens, (((1,), (1,)), ((), ())), preferred_element_type=jnp.float32
            )
            both.append(part.reshape(KF, 2 * ROWS_Y, 2 * PAIRS))
        joined = jnp.concatenate(both, axis=1).astype(jnp.bfloat16)
        sections[:, pl.ds(pl.multiple_of(j * 4 * ROWS_Y, 16), 4 * ROWS_Y), :] = joined
        return carry

    lax.fori_loop(0, LANES // CHUNK // 2, step, 0)
    for q in range(KF):
        out_ref[0, q] = jnp.dot(
            mix[...], sections[q], preferred_element_type=jnp.float32
        ).astype(jnp.bfloat16)


def densities(chosen, cond, z_mat, mix):
    planes = cond.shape[0]
    return pl.pallas_call(
        density_kernel,
        grid=(planes,),
        out_shape=jax.ShapeDtypeStruct((planes, KF, 2 * KF, 2 * PAIRS), jnp.bfloat16),
        in_specs=[
            pl.BlockSpec((2, 1, BLK, LANES), lambda i: (0, i, 0, 0)),
            pl.BlockSpec((1, BLK, LANES), lambda i: (i, 0, 0)),
            pl.BlockSpec(z_mat.shape, lambda i: (0, 0)),
            pl.BlockSpec(mix.shape, lambda i: (0, 0)),
        ],
        out_specs=pl.BlockSpec((1, KF, 2 * KF, 2 * PAIRS), lambda i: (i, 0, 0, 0)),
        scratch_shapes=[pltpu.VMEM((KF, 2 * GRID_N, 2 * PAIRS), jnp.bfloat16)],
        name="pair_density",
    )(chosen, cond, z_mat, mix)


def tail_kernel(
    devices, side_a, side_b, screened, out_ref, rows, parts, arrived,
    send, recv, own, sum_send, sum_recv,
):
    me = lax.axis_index("grid")
    half = devices // 2
    ring = half // 2
    z, y, c = me // half, me % half // 2, me % 2

    def at(zz, yy, cc):
        return zz * half + yy % ring * 2 + cc

    greet([{"grid": (me + k) % devices} for k in range(1, devices)])
    local = pltpu.make_async_copy(side_b, rows.at[me], own.at[0])
    local.start()
    started = []

    def push(slot, peer, from_input=False):
        copy = remote(
            side_b if from_input else rows.at[slot], rows.at[slot],
            send.at[len(started)], recv.at[slot], {"grid": peer},
        )
        copy.start()
        started.append(copy)

    def landed(slot):
        pltpu.make_async_remote_copy(
            src_ref=rows.at[slot], dst_ref=rows.at[slot], send_sem=own.at[0],
            recv_sem=recv.at[slot], device_id={"grid": at(z, y, 1 - c)}, device_id_type=MESH,
        ).wait_recv()

    up, down, twin = at(z, y + 1, c), at(z, y + ring - 1, c), at(z, y, 1 - c)
    push(me, at(1 - z, y, c), True)
    push(me, up, True)
    push(me, down, True)
    push(me, twin, True)
    other = at(1 - z, y, c)
    landed(other)
    push(other, up)
    push(other, down)
    push(other, twin)
    for t in range(1, ring // 2 + 1):
        for zz, ups in ((z, ring // 2), (1 - z, ring // 2 - 1)):
            for steps, back, peer in ((ups, ring - t, up), (ring - 1 - ups, t, down)):
                if t <= steps:
                    slot = at(zz, y + back, c)
                    landed(slot)
                    if t < steps:
                        push(slot, peer)
                    push(slot, twin)
    for zz in (z, 1 - z):
        for t in range(ring):
            landed(at(zz, y + t, 1 - c))
    local.wait()

    count = side_b.shape[0]

    def step(k, total):
        block = screened[:, pl.ds(pl.multiple_of(k * 2 * count, 128), 2 * count)]
        pair = rows[pl.ds(2 * k, 2)].reshape(2 * count, 2 * PAIRS)
        return total + jnp.dot(block, pair, preferred_element_type=jnp.float32)

    total = lax.fori_loop(0, half, step, jnp.zeros((count, 2 * PAIRS), jnp.float32))
    total = total.astype(jnp.bfloat16)
    product = lax.dot_general(
        side_a[...], total, (((0,), (0,)), ((), ())), preferred_element_type=jnp.float32
    )
    value = product[:PAIRS, :PAIRS] + product[PAIRS:, PAIRS:]
    width = PAIRS // devices
    for g in range(devices):
        parts[g] = value[g * width : (g + 1) * width]
    for copy in started:
        copy.wait_send()
    moves = []
    for k in range(1, devices):
        peer = (me + k) % devices
        copy = remote(
            parts.at[peer], arrived.at[k], sum_send.at[k], sum_recv.at[k], {"grid": peer}
        )
        copy.start()
        moves.append(copy)
    result = parts[me]
    for copy in moves:
        copy.wait()
    for k in range(1, devices):
        result = result + arrived[k]
    out_ref[...] = result


def tail(side_a, side_b, screened, devices):
    vmem = pl.BlockSpec(memory_space=pltpu.VMEM)
    dma = pltpu.SemaphoreType.DMA
    width = PAIRS // devices
    return pl.pallas_call(
        functools.partial(tail_kernel, devices),
        out_shape=jax.ShapeDtypeStruct((width, PAIRS), jnp.float32),
        in_specs=[vmem] * 3,
        out_specs=vmem,
        scratch_shapes=[
            pltpu.VMEM((devices, *side_b.shape), jnp.bfloat16),
            pltpu.VMEM((devices, width, PAIRS), jnp.float32),
            pltpu.VMEM((devices, width, PAIRS), jnp.float32),
            dma((devices,)), dma((devices,)), dma((1,)), dma((devices,)), dma((devices,)),
        ],
        compiler_params=pltpu.CompilerParams(collective_id=1, has_side_effects=True),
        name="screen_and_sum",
    )(side_a, side_b, screened)


def per_device(devices, valence, conduction, screened, blocks, gsphere):
    held_blocks = valence.shape[0] // BLK
    planes = conduction.shape[1]
    mix = jnp.asarray(mix_matrix())
    z_mat = jnp.asarray(z_matrix())
    by_plane = jnp.transpose(valence, (1, 0, 2))
    pieces = jnp.stack([
        lax.dynamic_slice_in_dim(by_plane, blocks[b] % held_blocks * BLK, BLK, 1) for b in range(2)
    ])
    chosen = spread(blocks // held_blocks, pieces)
    y_section = densities(chosen, jnp.transpose(conduction, (1, 0, 2)), z_mat, mix)
    blocks_y = y_section.reshape(planes, KF, KF, 2, 2 * PAIRS).transpose(2, 0, 3, 1, 4)
    moved = lax.all_to_all(blocks_y, "grid", split_axis=0, concat_axis=0, tiled=True)
    moved = moved.reshape(2 * GRID_N, KF, 2 * PAIRS)
    x_section = jnp.einsum(
        "kn,nqp->kqp", mix, moved, preferred_element_type=jnp.float32
    ).astype(jnp.bfloat16)
    flat = x_section.reshape(KF, 2, KF, 2 * PAIRS).transpose(0, 2, 1, 3).reshape(KF * KF, 2, 2 * PAIRS)
    sphere = jnp.take(flat, gsphere, axis=0)
    side_a = sphere[:, :, :PAIRS].reshape(-1, 2 * PAIRS)
    side_b = sphere[:, :, PAIRS:].reshape(-1, 2 * PAIRS)
    return tail(side_a, side_b, screened, devices)[None]


def solution(mesh):
    in_specs = (P("band", "grid", None), P("band", "grid", None), P("grid", None), P(), P("grid"))
    return jax.shard_map(
        functools.partial(per_device, mesh.shape["grid"]), mesh=mesh, in_specs=in_specs,
        out_specs=P("band", "grid", None), check_vma=False,
    )
```

```python
import functools
import math

import jax
import jax.numpy as jnp
import ml_dtypes
import numpy as np
from jax import lax
from jax.experimental import pallas as pl
from jax.experimental.pallas import tpu as pltpu
from jax.sharding import PartitionSpec as P

GRID_N = 96
KF = 32
BLK = 8
PAIRS = 64
SIDE = 4
LANES = GRID_N * GRID_N
PART = LANES // 2
PIECE = PART // SIDE
ROWS_Y = 4
CHUNK = ROWS_Y * GRID_N
NEG = KF // 2 + 1
FULL_X = KF + 1
ROWS_X = 48
MESH = pl.DeviceIdType.MESH


def fourier_parts(length, kept):
    positions = np.arange(length)
    freqs = np.arange(kept) - KF // 2
    phases = (positions[:, None] * freqs[None, :] % length) * (2.0 * math.pi / length)
    factor = 1.0 / math.sqrt(length)
    return np.cos(phases) * factor, np.sin(phases) * factor


def first_table():
    cosine, sine = fourier_parts(GRID_N, KF)
    return np.stack([cosine, -sine], axis=2)


def mixing_table(kept):
    cosine, sine = fourier_parts(GRID_N, kept)
    real_rows = np.stack([cosine, sine], axis=-1)
    imag_rows = np.stack([-sine, cosine], axis=-1)
    return np.stack([real_rows, imag_rows], axis=2)


def z_matrix():
    table = first_table()[:, :NEG]
    out = np.zeros((NEG, ROWS_Y, 2, ROWS_Y, GRID_N))
    for y in range(ROWS_Y):
        out[:, y, :, y, :] = np.transpose(table, (1, 2, 0))
    return out.reshape(NEG * ROWS_Y * 2, CHUNK).astype(ml_dtypes.bfloat16)


def y_matrix():
    table = np.transpose(mixing_table(KF), (1, 2, 0, 3))
    lowest = table[:1] * np.array([1.0, -1.0])
    return np.concatenate([table, lowest]).reshape(2 * KF + 2, 2 * GRID_N).astype(ml_dtypes.bfloat16)


def x_matrix():
    table = np.transpose(mixing_table(FULL_X), (2, 1, 0, 3)).reshape(2, FULL_X, 2 * GRID_N)
    out = np.zeros((2, ROWS_X, 2 * GRID_N))
    out[:, :FULL_X] = table
    return out.reshape(2 * ROWS_X, 2 * GRID_N).astype(ml_dtypes.bfloat16)


def remote(src, dst, send, recv, peer):
    return pltpu.make_async_remote_copy(
        src_ref=src, dst_ref=dst, send_sem=send, recv_sem=recv, device_id=peer, device_id_type=MESH
    )


def greet(peers):
    barrier = pltpu.get_barrier_semaphore()
    for peer in peers:
        pl.semaphore_signal(barrier, inc=1, device_id=peer, device_id_type=MESH)
    pl.semaphore_wait(barrier, len(peers))


def spread_kernel(
    owner_ref, src, out_ref, near0, near1, near2, near3, held, far, mine, full,
    send1, recv1, own1, send2, recv2, send3, recv3, send4, recv4,
):
    band = lax.axis_index("band")
    z, x = band // SIDE, band % SIDE
    near = (near0, near1, near2, near3)

    def along_x(k):
        return {"band": z * SIDE + (x + k) % SIDE}

    def along_z(k):
        return {"band": (z + k) % SIDE * SIDE + x}

    def lanes(q, s):
        return pl.ds(pl.multiple_of(q % 2 * PART + s * PIECE, 128), PIECE)

    greet([along_x(k) for k in (1, 2, 3)] + [along_z(k) for k in (1, 2, 3)])
    order = (2, 1, 3, 0)
    first = {}
    for j in order:
        s = (z + j) % SIDE
        for k in (2, 1, 3):
            q = (x + k) % SIDE
            copy = remote(
                src.at[q // 2, :, :, lanes(q, s)], near[j].at[x],
                send1.at[j, k - 1], recv1.at[j, k - 1], along_x(k),
            )
            copy.start()
            first[j, k] = copy
        copy = pltpu.make_async_copy(src.at[x // 2, :, :, lanes(x, s)], near[j].at[x], own1.at[j])
        copy.start()
        first[j, 0] = copy
    owner = owner_ref[x // 2]
    owner_z, owner_x = owner // SIDE, owner % SIDE
    second = []
    for j in order:
        for k in range(SIDE):
            first[j, k].wait()
        if j == 0:
            far[z] = near[j][owner_x]
        else:
            held[j] = near[j][owner_x]
            copy = remote(
                held.at[j], far.at[z], send2.at[j - 1], recv2.at[j - 1], along_z(j)
            )
            copy.start()
            second.append(copy)
    for copy in second:
        copy.wait()
    picked = far[owner_z]
    mine[...] = picked
    full[x // 2, :, :, lanes(x, z)] = picked
    third = {}
    for k in (2, 1, 3):
        copy = remote(
            mine, full.at[x // 2, :, :, lanes(x, z)], send3.at[k - 1], recv3.at[k - 1], along_z(k)
        )
        copy.start()
        third[k] = copy
    fourth = []
    for j in (0, 1, 3, 2):
        if j:
            third[j].wait()
        s = (z + SIDE - j) % SIDE
        part = full.at[x // 2, :, :, lanes(x, s)]
        for k in (2, 1, 3):
            copy = remote(
                mine if j == 0 else part, part, send4.at[j, k - 1], recv4.at[j, k - 1], along_x(k)
            )
            copy.start()
            fourth.append(copy)
    for copy in fourth:
        copy.wait()
    out_ref[...] = full[...]


def spread(owner, pieces):
    piece = (3, BLK, PIECE)
    dma = pltpu.SemaphoreType.DMA
    vmem = pl.BlockSpec(memory_space=pltpu.VMEM)
    return pl.pallas_call(
        spread_kernel,
        out_shape=jax.ShapeDtypeStruct(pieces.shape, pieces.dtype),
        in_specs=[pl.BlockSpec(memory_space=pltpu.SMEM), vmem],
        out_specs=vmem,
        scratch_shapes=[
            *[pltpu.VMEM((SIDE, *piece), jnp.bfloat16) for _ in range(SIDE)],
            pltpu.VMEM((SIDE, *piece), jnp.bfloat16),
            pltpu.VMEM((SIDE, *piece), jnp.bfloat16),
            pltpu.VMEM(piece, jnp.bfloat16),
            pltpu.VMEM(pieces.shape, jnp.bfloat16),
            dma((SIDE, 3)), dma((SIDE, 3)), dma((SIDE,)),
            dma((3,)), dma((3,)), dma((3,)), dma((3,)),
            dma((SIDE, 3)), dma((SIDE, 3)),
        ],
        compiler_params=pltpu.CompilerParams(collective_id=0, has_side_effects=True),
        name="spread_blocks",
    )(owner, pieces)


def density_kernel(chosen, cond, z_mat, mix, out_ref, sections):
    def step(j, carry):
        both = []
        for half in range(2):
            at = pl.ds(pl.multiple_of((2 * j + half) * CHUNK, 128), CHUNK)
            c = cond[0, :, at].astype(jnp.float32)
            v = jnp.concatenate(
                [chosen[0, 0, :, at].astype(jnp.float32), chosen[1, 0, :, at].astype(jnp.float32)]
            )
            dens = (v[:, None, :] * c[None, :, :]).reshape(2 * PAIRS, CHUNK).astype(jnp.bfloat16)
            part = lax.dot_general(
                z_mat[...], dens, (((1,), (1,)), ((), ())), preferred_element_type=jnp.float32
            )
            both.append(part.reshape(NEG, 2 * ROWS_Y, 2 * PAIRS))
        joined = jnp.concatenate(both, axis=1).astype(jnp.bfloat16)
        sections[:, pl.ds(pl.multiple_of(j * 4 * ROWS_Y, 16), 4 * ROWS_Y), :] = joined
        return carry

    lax.fori_loop(0, LANES // CHUNK // 2, step, 0)
    for q in range(NEG):
        out_ref[0, q] = jnp.dot(
            mix[...], sections[q], preferred_element_type=jnp.float32
        ).astype(jnp.bfloat16)


def densities(chosen, cond, z_mat, mix):
    planes = cond.shape[0]
    return pl.pallas_call(
        density_kernel,
        grid=(planes,),
        out_shape=jax.ShapeDtypeStruct((planes, NEG, 2 * KF + 2, 2 * PAIRS), jnp.bfloat16),
        in_specs=[
            pl.BlockSpec((2, 1, BLK, LANES), lambda i: (0, i, 0, 0)),
            pl.BlockSpec((1, BLK, LANES), lambda i: (i, 0, 0)),
            pl.BlockSpec(z_mat.shape, lambda i: (0, 0)),
            pl.BlockSpec(mix.shape, lambda i: (0, 0)),
        ],
        out_specs=pl.BlockSpec((1, NEG, 2 * KF + 2, 2 * PAIRS), lambda i: (i, 0, 0, 0)),
        scratch_shapes=[pltpu.VMEM((NEG, 2 * GRID_N, 2 * PAIRS), jnp.bfloat16)],
        name="pair_density",
    )(chosen, cond, z_mat, mix)


def one_hot(index, count):
    lanes = lax.broadcasted_iota(jnp.int32, (index.shape[0], count), 1)
    return jnp.where(lanes == index, 1.0, 0.0).astype(jnp.bfloat16)


def sphere_kernel(moved, mix, own_at, twin_at, own_ref, twin_ref, table_ref, table):
    for q in range(NEG + 1):
        part = jnp.dot(mix[...], moved[q], preferred_element_type=jnp.float32)
        both = jnp.concatenate([part[:ROWS_X], part[ROWS_X:]], axis=1).astype(jnp.bfloat16)
        if q < NEG:
            table[q * ROWS_X : (q + 1) * ROWS_X] = both
        else:
            table_ref[...] = both[:KF]
    count = table.shape[0]
    own = jnp.dot(one_hot(own_at[...], count), table[...], preferred_element_type=jnp.float32)
    own_ref[...] = own.astype(jnp.bfloat16)
    twin = jnp.dot(one_hot(twin_at[...], count), table[...], preferred_element_type=jnp.float32)
    lanes = lax.broadcasted_iota(jnp.int32, twin.shape, 1)
    twin_ref[...] = jnp.where(lanes < 2 * PAIRS, twin, -twin).astype(jnp.bfloat16)


def spheres(moved, mix, own_at, twin_at):
    rows = jax.ShapeDtypeStruct((own_at.shape[0], 4 * PAIRS), jnp.bfloat16)
    vmem = pl.BlockSpec(memory_space=pltpu.VMEM)
    return pl.pallas_call(
        sphere_kernel,
        out_shape=[rows, rows, jax.ShapeDtypeStruct((KF, 4 * PAIRS), jnp.bfloat16)],
        in_specs=[vmem] * 4,
        out_specs=[vmem] * 3,
        scratch_shapes=[pltpu.VMEM((NEG * ROWS_X, 4 * PAIRS), jnp.bfloat16)],
        name="x_and_sphere",
    )(moved, mix, own_at, twin_at)


def tail_kernel(
    devices, own_rows, twin_rows, table, lone_at, screened, out_ref,
    got, tables, side_a, side_b, rows, parts, arrived,
    swap_send, swap_recv, lone_send, lone_recv, send, recv, own, sum_send, sum_recv,
):
    me = lax.axis_index("grid")
    half = devices // 2
    ring = half // 2
    z, y, c = me // half, me % half // 2, me % 2

    def at(zz, yy, cc):
        return zz * half + yy % ring * 2 + cc

    greet([{"grid": (me + k) % devices} for k in range(1, devices)])
    paired = (me != 0) & (me != half)
    swap = remote(
        twin_rows, got, swap_send.at[0], swap_recv.at[0], {"grid": (devices - me) % devices}
    )
    helper = (me > 0) & (me < half)

    @pl.when(helper)
    def _():
        remote(
            table, tables.at[me - 1], lone_send.at[0], lone_recv.at[me - 1], {"grid": 0}
        ).start()

    @pl.when(paired)
    def _():
        swap.start()
        swap.wait()

    @pl.when(me == half)
    def _():
        got[...] = twin_rows[...]

    @pl.when(me == 0)
    def _():
        for i in range(half - 1):
            remote(
                table, tables.at[i], lone_send.at[0], lone_recv.at[i], {"grid": i + 1}
            ).wait_recv()
        count = (half - 1) * KF
        picked = jnp.dot(
            one_hot(lone_at[...], count), tables[...].reshape(count, 4 * PAIRS),
            preferred_element_type=jnp.float32,
        )
        got[...] = picked.astype(jnp.bfloat16)

    @pl.when(helper)
    def _():
        remote(
            table, tables.at[me - 1], lone_send.at[0], lone_recv.at[me - 1], {"grid": 0}
        ).wait_send()

    sphere = own_rows[...].astype(jnp.float32) + got[...].astype(jnp.float32)
    real, imag = sphere[:, : 2 * PAIRS], sphere[:, 2 * PAIRS :]
    side_b[...] = jnp.concatenate([real[:, PAIRS:], imag[:, PAIRS:]], axis=1).astype(jnp.bfloat16)
    side_a[...] = jnp.concatenate([real[:, :PAIRS], imag[:, :PAIRS]], axis=1).astype(jnp.bfloat16)
    local = pltpu.make_async_copy(side_b, rows.at[me], own.at[0])
    local.start()
    started = []

    def push(slot, peer, from_input=False):
        copy = remote(
            side_b if from_input else rows.at[slot], rows.at[slot],
            send.at[len(started)], recv.at[slot], {"grid": peer},
        )
        copy.start()
        started.append(copy)

    def landed(slot):
        pltpu.make_async_remote_copy(
            src_ref=rows.at[slot], dst_ref=rows.at[slot], send_sem=own.at[0],
            recv_sem=recv.at[slot], device_id={"grid": at(z, y, 1 - c)}, device_id_type=MESH,
        ).wait_recv()

    up, down, twin = at(z, y + 1, c), at(z, y + ring - 1, c), at(z, y, 1 - c)
    push(me, at(1 - z, y, c), True)
    push(me, up, True)
    push(me, down, True)
    push(me, twin, True)
    other = at(1 - z, y, c)
    landed(other)
    push(other, up)
    push(other, down)
    push(other, twin)
    for t in range(1, ring // 2 + 1):
        for zz, ups in ((z, ring // 2), (1 - z, ring // 2 - 1)):
            for steps, back, peer in ((ups, ring - t, up), (ring - 1 - ups, t, down)):
                if t <= steps:
                    slot = at(zz, y + back, c)
                    landed(slot)
                    if t < steps:
                        push(slot, peer)
                    push(slot, twin)
    for zz in (z, 1 - z):
        for t in range(ring):
            landed(at(zz, y + t, 1 - c))
    local.wait()

    count = side_b.shape[0]

    def step(k, total):
        block = screened[:, pl.ds(pl.multiple_of(k * 2 * count, 128), 2 * count)]
        pair = rows[pl.ds(2 * k, 2)].reshape(2 * count, 2 * PAIRS)
        return total + jnp.dot(block, pair, preferred_element_type=jnp.float32)

    total = lax.fori_loop(0, half, step, jnp.zeros((count, 2 * PAIRS), jnp.float32))
    total = total.astype(jnp.bfloat16)
    product = lax.dot_general(
        side_a[...], total, (((0,), (0,)), ((), ())), preferred_element_type=jnp.float32
    )
    value = product[:PAIRS, :PAIRS] + product[PAIRS:, PAIRS:]
    width = PAIRS // devices
    for g in range(devices):
        parts[g] = value[g * width : (g + 1) * width]
    for copy in started:
        copy.wait_send()
    moves = []
    for k in range(1, devices):
        peer = (me + k) % devices
        copy = remote(
            parts.at[peer], arrived.at[k], sum_send.at[k], sum_recv.at[k], {"grid": peer}
        )
        copy.start()
        moves.append(copy)
    result = parts[me]
    for copy in moves:
        copy.wait()
    for k in range(1, devices):
        result = result + arrived[k]
    out_ref[...] = result


def tail(own_rows, twin_rows, table, lone_at, screened, devices):
    vmem = pl.BlockSpec(memory_space=pltpu.VMEM)
    dma = pltpu.SemaphoreType.DMA
    width = PAIRS // devices
    side = (own_rows.shape[0], 2 * PAIRS)
    return pl.pallas_call(
        functools.partial(tail_kernel, devices),
        out_shape=jax.ShapeDtypeStruct((width, PAIRS), jnp.float32),
        in_specs=[vmem] * 5,
        out_specs=vmem,
        scratch_shapes=[
            pltpu.VMEM(own_rows.shape, jnp.bfloat16),
            pltpu.VMEM((devices // 2 - 1, *table.shape), jnp.bfloat16),
            pltpu.VMEM(side, jnp.bfloat16),
            pltpu.VMEM(side, jnp.bfloat16),
            pltpu.VMEM((devices, *side), jnp.bfloat16),
            pltpu.VMEM((devices, width, PAIRS), jnp.float32),
            pltpu.VMEM((devices, width, PAIRS), jnp.float32),
            dma((1,)), dma((1,)), dma((1,)), dma((devices // 2 - 1,)),
            dma((devices,)), dma((devices,)), dma((1,)), dma((devices,)), dma((devices,)),
        ],
        compiler_params=pltpu.CompilerParams(collective_id=1, has_side_effects=True),
        name="screen_and_sum",
    )(own_rows, twin_rows, table, lone_at, screened)


def per_device(devices, valence, conduction, screened, blocks, gsphere):
    held_blocks = valence.shape[0] // BLK
    planes = conduction.shape[1]
    twin_points = lax.ppermute(
        gsphere, "grid", [(g, (devices - g) % devices) for g in range(devices)]
    )
    by_plane = jnp.transpose(valence, (1, 0, 2))
    pieces = jnp.stack([
        lax.dynamic_slice_in_dim(by_plane, blocks[b] % held_blocks * BLK, BLK, 1) for b in range(2)
    ])
    chosen = spread(blocks // held_blocks, pieces)
    y_section = densities(
        chosen, jnp.transpose(conduction, (1, 0, 2)), jnp.asarray(z_matrix()), jnp.asarray(y_matrix())
    )
    blocks_y = y_section[:, :, : 2 * KF].reshape(planes, NEG, KF, 2, 2 * PAIRS)
    lowest = jnp.flip(y_section[:, :, 2 * KF :], axis=1)
    lowest = jnp.pad(lowest, ((0, 0), (0, KF - NEG), (0, 0), (0, 0)))
    blocks_y = jnp.concatenate([blocks_y, lowest[:, None]], axis=1).transpose(2, 0, 3, 1, 4)
    moved = lax.all_to_all(blocks_y, "grid", split_axis=0, concat_axis=0, tiled=True)
    moved = moved.reshape(2 * GRID_N, NEG + 1, 2 * PAIRS).transpose(1, 0, 2)
    qx, qz = gsphere // KF, gsphere % KF
    twin_qx, twin_qz = twin_points // KF, twin_points % KF
    own_at = jnp.where(qz < NEG, qz * ROWS_X + qx, -1)[:, None]
    lone_at = jnp.where(qz < NEG, -1, (qz - NEG) * KF + qx)[:, None]
    twin_at = jnp.where(twin_qz < NEG, -1, (KF - twin_qz) * ROWS_X + KF - twin_qx)[:, None]
    own_rows, twin_rows, table = spheres(moved, jnp.asarray(x_matrix()), own_at, twin_at)
    return tail(own_rows, twin_rows, table, lone_at, screened, devices)[None]


def solution(mesh):
    in_specs = (P("band", "grid", None), P("band", "grid", None), P("grid", None), P(), P("grid"))
    return jax.shard_map(
        functools.partial(per_device, mesh.shape["grid"]), mesh=mesh, in_specs=in_specs,
        out_specs=P("band", "grid", None), check_vma=False,
    )
```

```python
import functools
import math

import jax
import jax.numpy as jnp
import ml_dtypes
import numpy as np
from jax import lax
from jax.experimental import pallas as pl
from jax.experimental.pallas import tpu as pltpu
from jax.sharding import PartitionSpec as P

GRID_N = 96
KF = 32
BLK = 8
PAIRS = 64
SIDE = 4
LANES = GRID_N * GRID_N
PART = LANES // 2
PIECE = PART // SIDE
ROWS_Y = 4
CHUNK = ROWS_Y * GRID_N
NEG = KF // 2 + 1
FULL_X = KF + 1
ROWS_X = 48
MESH = pl.DeviceIdType.MESH


def fourier_parts(length, kept):
    positions = np.arange(length)
    freqs = np.arange(kept) - KF // 2
    phases = (positions[:, None] * freqs[None, :] % length) * (2.0 * math.pi / length)
    factor = 1.0 / math.sqrt(length)
    return np.cos(phases) * factor, np.sin(phases) * factor


def first_table():
    cosine, sine = fourier_parts(GRID_N, KF)
    return np.stack([cosine, -sine], axis=2)


def mixing_table(kept):
    cosine, sine = fourier_parts(GRID_N, kept)
    real_rows = np.stack([cosine, sine], axis=-1)
    imag_rows = np.stack([-sine, cosine], axis=-1)
    return np.stack([real_rows, imag_rows], axis=2)


def z_matrix():
    table = first_table()[:, :NEG]
    out = np.zeros((NEG, ROWS_Y, 2, ROWS_Y, GRID_N))
    for y in range(ROWS_Y):
        out[:, y, :, y, :] = np.transpose(table, (1, 2, 0))
    return out.reshape(NEG * ROWS_Y * 2, CHUNK).astype(ml_dtypes.bfloat16)


def y_matrix():
    table = np.transpose(mixing_table(KF), (1, 2, 0, 3))
    lowest = table[:1] * np.array([1.0, -1.0])
    return np.concatenate([table, lowest]).reshape(2 * KF + 2, 2 * GRID_N).astype(ml_dtypes.bfloat16)


def x_matrix():
    table = np.transpose(mixing_table(FULL_X), (2, 1, 0, 3)).reshape(2, FULL_X, 2 * GRID_N)
    out = np.zeros((2, ROWS_X, 2 * GRID_N))
    out[:, :FULL_X] = table
    return out.reshape(2 * ROWS_X, 2 * GRID_N).astype(ml_dtypes.bfloat16)


def remote(src, dst, send, recv, peer):
    return pltpu.make_async_remote_copy(
        src_ref=src, dst_ref=dst, send_sem=send, recv_sem=recv, device_id=peer, device_id_type=MESH
    )


def greet(peers):
    barrier = pltpu.get_barrier_semaphore()
    for peer in peers:
        pl.semaphore_signal(barrier, inc=1, device_id=peer, device_id_type=MESH)
    pl.semaphore_wait(barrier, len(peers))


def spread_kernel(
    blocks_ref, held_bands, out_ref, src, near0, near1, near2, near3, held, far, mine, full,
    send1, recv1, own1, send2, recv2, send3, recv3, send4, recv4,
):
    band = lax.axis_index("band")
    z, x = band // SIDE, band % SIDE
    near = (near0, near1, near2, near3)

    def along_x(k):
        return {"band": z * SIDE + (x + k) % SIDE}

    def along_z(k):
        return {"band": (z + k) % SIDE * SIDE + x}

    def lanes(q, s):
        return pl.ds(pl.multiple_of(q % 2 * PART + s * PIECE, 128), PIECE)

    count = held_bands.shape[1]
    for b in range(2):
        src[b] = held_bands[:, lax.rem(blocks_ref[b], count)]
    greet([along_x(k) for k in (1, 2, 3)] + [along_z(k) for k in (1, 2, 3)])
    order = (2, 1, 3, 0)
    first = {}
    for j in order:
        s = (z + j) % SIDE
        for k in (2, 1, 3):
            q = (x + k) % SIDE
            copy = remote(
                src.at[q // 2, :, :, lanes(q, s)], near[j].at[x],
                send1.at[j, k - 1], recv1.at[j, k - 1], along_x(k),
            )
            copy.start()
            first[j, k] = copy
        copy = pltpu.make_async_copy(src.at[x // 2, :, :, lanes(x, s)], near[j].at[x], own1.at[j])
        copy.start()
        first[j, 0] = copy
    owner = lax.div(blocks_ref[x // 2], count)
    owner_z, owner_x = owner // SIDE, owner % SIDE
    second = []
    for j in order:
        for k in range(SIDE):
            first[j, k].wait()
        if j == 0:
            far[z] = near[j][owner_x]
        else:
            held[j] = near[j][owner_x]
            copy = remote(
                held.at[j], far.at[z], send2.at[j - 1], recv2.at[j - 1], along_z(j)
            )
            copy.start()
            second.append(copy)
    for copy in second:
        copy.wait()
    picked = far[owner_z]
    mine[...] = picked
    full[x // 2, :, :, lanes(x, z)] = picked
    third = {}
    for k in (2, 1, 3):
        copy = remote(
            mine, full.at[x // 2, :, :, lanes(x, z)], send3.at[k - 1], recv3.at[k - 1], along_z(k)
        )
        copy.start()
        third[k] = copy
    fourth = []
    for j in (0, 1, 3, 2):
        if j:
            third[j].wait()
        s = (z + SIDE - j) % SIDE
        part = full.at[x // 2, :, :, lanes(x, s)]
        for k in (2, 1, 3):
            copy = remote(
                mine if j == 0 else part, part, send4.at[j, k - 1], recv4.at[j, k - 1], along_x(k)
            )
            copy.start()
            fourth.append(copy)
    for copy in fourth:
        copy.wait()
    out_ref[...] = full[...]


def spread(blocks, held_bands):
    planes = held_bands.shape[0]
    whole = (2, planes, BLK, LANES)
    piece = (planes, BLK, PIECE)
    dma = pltpu.SemaphoreType.DMA
    vmem = pl.BlockSpec(memory_space=pltpu.VMEM)
    return pl.pallas_call(
        spread_kernel,
        out_shape=jax.ShapeDtypeStruct(whole, jnp.bfloat16),
        in_specs=[pl.BlockSpec(memory_space=pltpu.SMEM), vmem],
        out_specs=vmem,
        scratch_shapes=[
            pltpu.VMEM(whole, jnp.bfloat16),
            *[pltpu.VMEM((SIDE, *piece), jnp.bfloat16) for _ in range(SIDE)],
            pltpu.VMEM((SIDE, *piece), jnp.bfloat16),
            pltpu.VMEM((SIDE, *piece), jnp.bfloat16),
            pltpu.VMEM(piece, jnp.bfloat16),
            pltpu.VMEM(whole, jnp.bfloat16),
            dma((SIDE, 3)), dma((SIDE, 3)), dma((SIDE,)),
            dma((3,)), dma((3,)), dma((3,)), dma((3,)),
            dma((SIDE, 3)), dma((SIDE, 3)),
        ],
        compiler_params=pltpu.CompilerParams(collective_id=0, has_side_effects=True),
        name="spread_blocks",
    )(blocks, held_bands)


def density_kernel(chosen, cond, z_mat, mix, out_ref, sections):
    def step(j, carry):
        both = []
        for half in range(2):
            at = pl.ds(pl.multiple_of((2 * j + half) * CHUNK, 128), CHUNK)
            c = cond[0, :, at].astype(jnp.float32)
            v = jnp.concatenate(
                [chosen[0, 0, :, at].astype(jnp.float32), chosen[1, 0, :, at].astype(jnp.float32)]
            )
            dens = (v[:, None, :] * c[None, :, :]).reshape(2 * PAIRS, CHUNK).astype(jnp.bfloat16)
            part = lax.dot_general(
                z_mat[...], dens, (((1,), (1,)), ((), ())), preferred_element_type=jnp.float32
            )
            both.append(part.reshape(NEG, 2 * ROWS_Y, 2 * PAIRS))
        joined = jnp.concatenate(both, axis=1).astype(jnp.bfloat16)
        sections[:, pl.ds(pl.multiple_of(j * 4 * ROWS_Y, 16), 4 * ROWS_Y), :] = joined
        return carry

    lax.fori_loop(0, LANES // CHUNK // 2, step, 0)
    for q in range(NEG):
        out_ref[0, q] = jnp.dot(
            mix[...], sections[q], preferred_element_type=jnp.float32
        ).astype(jnp.bfloat16)


def densities(chosen, cond, z_mat, mix):
    planes = cond.shape[0]
    return pl.pallas_call(
        density_kernel,
        grid=(planes,),
        out_shape=jax.ShapeDtypeStruct((planes, NEG, 2 * KF + 2, 2 * PAIRS), jnp.bfloat16),
        in_specs=[
            pl.BlockSpec((2, 1, BLK, LANES), lambda i: (0, i, 0, 0)),
            pl.BlockSpec((1, BLK, LANES), lambda i: (i, 0, 0)),
            pl.BlockSpec(z_mat.shape, lambda i: (0, 0)),
            pl.BlockSpec(mix.shape, lambda i: (0, 0)),
        ],
        out_specs=pl.BlockSpec((1, NEG, 2 * KF + 2, 2 * PAIRS), lambda i: (i, 0, 0, 0)),
        scratch_shapes=[pltpu.VMEM((NEG, 2 * GRID_N, 2 * PAIRS), jnp.bfloat16)],
        name="pair_density",
    )(chosen, cond, z_mat, mix)


def exchange_kernel(devices, src, out_ref, kept, send, recv, own):
    me = lax.axis_index("grid")
    half = devices // 2
    ring = half // 2
    z, y, c = me // half, me % half // 2, me % 2
    greet([{"grid": (me + k) % devices} for k in range(1, devices)])
    inward = pltpu.make_async_copy(src.at[me], kept, own.at[0])
    inward.start()
    moves = []
    for dy in sorted(range(ring), key=lambda d: -min(d, ring - d)):
        for dz in (1, 0):
            for dc in (0, 1):
                k = dz * half + dy * 2 + dc
                if k:
                    peer = (z + dz) % 2 * half + (y + dy) % ring * 2 + (c + dc) % 2
                    copy = remote(
                        src.at[peer], out_ref.at[me], send.at[k], recv.at[k], {"grid": peer}
                    )
                    copy.start()
                    moves.append((dy, dz, dc, k, copy))
    inward.wait()
    outward = pltpu.make_async_copy(kept, out_ref.at[me], own.at[1])
    outward.start()
    for dy, dz, dc, k, copy in moves:
        copy.wait_send()
        peer = (z + dz) % 2 * half + (y + ring - dy) % ring * 2 + (c + dc) % 2
        remote(src.at[peer], out_ref.at[peer], send.at[k], recv.at[k], {"grid": peer}).wait_recv()
    outward.wait()


def exchange(blocks, devices):
    dma = pltpu.SemaphoreType.DMA
    return pl.pallas_call(
        functools.partial(exchange_kernel, devices),
        out_shape=jax.ShapeDtypeStruct(blocks.shape, blocks.dtype),
        in_specs=[pl.BlockSpec(memory_space=pl.ANY)],
        out_specs=pl.BlockSpec(memory_space=pl.ANY),
        scratch_shapes=[
            pltpu.VMEM(blocks.shape[1:], blocks.dtype), dma((devices,)), dma((devices,)), dma((2,))
        ],
        compiler_params=pltpu.CompilerParams(collective_id=2, has_side_effects=True),
        name="planes_for_frequencies",
    )(blocks)


def one_hot(index, count):
    lanes = lax.broadcasted_iota(jnp.int32, (index.shape[0], count), 1)
    return jnp.where(lanes == index, 1.0, 0.0).astype(jnp.bfloat16)


def sphere_kernel(moved, mix, own_at, twin_at, own_ref, twin_ref, table_ref, table):
    for q in range(NEG + 1):
        part = jnp.dot(mix[...], moved[q], preferred_element_type=jnp.float32)
        both = jnp.concatenate([part[:ROWS_X], part[ROWS_X:]], axis=1).astype(jnp.bfloat16)
        if q < NEG:
            table[q * ROWS_X : (q + 1) * ROWS_X] = both
        else:
            table_ref[...] = both[:KF]
    count = table.shape[0]
    own = jnp.dot(one_hot(own_at[...], count), table[...], preferred_element_type=jnp.float32)
    own_ref[...] = own.astype(jnp.bfloat16)
    twin = jnp.dot(one_hot(twin_at[...], count), table[...], preferred_element_type=jnp.float32)
    lanes = lax.broadcasted_iota(jnp.int32, twin.shape, 1)
    twin_ref[...] = jnp.where(lanes < 2 * PAIRS, twin, -twin).astype(jnp.bfloat16)


def spheres(moved, mix, own_at, twin_at):
    rows = jax.ShapeDtypeStruct((own_at.shape[0], 4 * PAIRS), jnp.bfloat16)
    vmem = pl.BlockSpec(memory_space=pltpu.VMEM)
    return pl.pallas_call(
        sphere_kernel,
        out_shape=[rows, rows, jax.ShapeDtypeStruct((KF, 4 * PAIRS), jnp.bfloat16)],
        in_specs=[vmem] * 4,
        out_specs=[vmem] * 3,
        scratch_shapes=[pltpu.VMEM((NEG * ROWS_X, 4 * PAIRS), jnp.bfloat16)],
        name="x_and_sphere",
    )(moved, mix, own_at, twin_at)


def tail_kernel(
    devices, own_rows, twin_rows, table, lone_at, screened, out_ref,
    weights, total, got, tables, side_a, side_b, rows, parts, arrived,
    swap_send, swap_recv, lone_send, lone_recv, send, recv, own, sum_send, sum_recv, fetched,
):
    fetch = pltpu.make_async_copy(screened, weights, fetched.at[0])
    fetch.start()
    me = lax.axis_index("grid")
    half = devices // 2
    ring = half // 2
    z, y, c = me // half, me % half // 2, me % 2

    def at(zz, yy, cc):
        return zz * half + yy % ring * 2 + cc

    greet([{"grid": (me + k) % devices} for k in range(1, devices)])
    paired = (me != 0) & (me != half)
    swap = remote(
        twin_rows, got, swap_send.at[0], swap_recv.at[0], {"grid": (devices - me) % devices}
    )
    helper = (me > 0) & (me < half)

    @pl.when(helper)
    def _():
        remote(
            table, tables.at[me - 1], lone_send.at[0], lone_recv.at[me - 1], {"grid": 0}
        ).start()

    @pl.when(paired)
    def _():
        swap.start()
        swap.wait()

    @pl.when(me == half)
    def _():
        got[...] = twin_rows[...]

    @pl.when(me == 0)
    def _():
        for i in range(half - 1):
            remote(
                table, tables.at[i], lone_send.at[0], lone_recv.at[i], {"grid": i + 1}
            ).wait_recv()
        count = (half - 1) * KF
        picked = jnp.dot(
            one_hot(lone_at[...], count), tables[...].reshape(count, 4 * PAIRS),
            preferred_element_type=jnp.float32,
        )
        got[...] = picked.astype(jnp.bfloat16)

    @pl.when(helper)
    def _():
        remote(
            table, tables.at[me - 1], lone_send.at[0], lone_recv.at[me - 1], {"grid": 0}
        ).wait_send()

    sphere = own_rows[...].astype(jnp.float32) + got[...].astype(jnp.float32)
    real, imag = sphere[:, : 2 * PAIRS], sphere[:, 2 * PAIRS :]
    side_b[...] = jnp.concatenate([real[:, PAIRS:], imag[:, PAIRS:]], axis=1).astype(jnp.bfloat16)
    side_a[...] = jnp.concatenate([real[:, :PAIRS], imag[:, :PAIRS]], axis=1).astype(jnp.bfloat16)
    local = pltpu.make_async_copy(side_b, rows.at[me], own.at[0])
    local.start()
    started = []

    def push(slot, peer, from_input=False):
        copy = remote(
            side_b if from_input else rows.at[slot], rows.at[slot],
            send.at[len(started)], recv.at[slot], {"grid": peer},
        )
        copy.start()
        started.append(copy)

    def landed(slot):
        pltpu.make_async_remote_copy(
            src_ref=rows.at[slot], dst_ref=rows.at[slot], send_sem=own.at[0],
            recv_sem=recv.at[slot], device_id={"grid": at(z, y, 1 - c)}, device_id_type=MESH,
        ).wait_recv()

    up, down, twin = at(z, y + 1, c), at(z, y + ring - 1, c), at(z, y, 1 - c)
    push(me, at(1 - z, y, c), True)
    push(me, up, True)
    push(me, down, True)
    push(me, twin, True)
    other = at(1 - z, y, c)
    landed(other)
    push(other, up)
    push(other, down)
    push(other, twin)
    count = side_a.shape[0]
    total[...] = jnp.zeros_like(total)
    local.wait()
    fetch.wait()

    def screen(zz, back):
        landed(at(zz, y + back, 1 - c))
        first = at(zz, y + back, 0)
        columns = pl.ds(pl.multiple_of(first * count, 128), 2 * count)
        pair = rows[pl.ds(first, 2)].reshape(2 * count, 2 * PAIRS)
        total[...] += jnp.dot(weights[:, columns], pair, preferred_element_type=jnp.float32)

    ready = [(z, 0), (1 - z, 0)]
    for t in range(1, ring // 2 + 1):
        fresh = []
        for zz, ups in ((z, ring // 2), (1 - z, ring // 2 - 1)):
            for steps, back, peer in ((ups, ring - t, up), (ring - 1 - ups, t, down)):
                if t <= steps:
                    slot = at(zz, y + back, c)
                    landed(slot)
                    if t < steps:
                        push(slot, peer)
                    push(slot, twin)
                    fresh.append((zz, back))
        for pair in ready:
            screen(*pair)
        ready = fresh
    for pair in ready:
        screen(*pair)
    product = lax.dot_general(
        side_a[...], total[...].astype(jnp.bfloat16), (((0,), (0,)), ((), ())), preferred_element_type=jnp.float32
    )
    value = product[:PAIRS, :PAIRS] + product[PAIRS:, PAIRS:]
    width = PAIRS // devices
    for g in range(devices):
        parts[g] = value[g * width : (g + 1) * width]
    for copy in started:
        copy.wait_send()
    moves = []
    for k in range(1, devices):
        peer = (me + k) % devices
        copy = remote(
            parts.at[peer], arrived.at[k], sum_send.at[k], sum_recv.at[k], {"grid": peer}
        )
        copy.start()
        moves.append(copy)
    result = parts[me]
    for copy in moves:
        copy.wait()
    for k in range(1, devices):
        result = result + arrived[k]
    out_ref[...] = result


def tail(own_rows, twin_rows, table, lone_at, screened, devices):
    vmem = pl.BlockSpec(memory_space=pltpu.VMEM)
    dma = pltpu.SemaphoreType.DMA
    width = PAIRS // devices
    side = (own_rows.shape[0], 2 * PAIRS)
    return pl.pallas_call(
        functools.partial(tail_kernel, devices),
        out_shape=jax.ShapeDtypeStruct((width, PAIRS), jnp.float32),
        in_specs=[vmem] * 4 + [pl.BlockSpec(memory_space=pl.ANY)],
        out_specs=vmem,
        scratch_shapes=[
            pltpu.VMEM(screened.shape, jnp.bfloat16),
            pltpu.VMEM(side, jnp.float32),
            pltpu.VMEM(own_rows.shape, jnp.bfloat16),
            pltpu.VMEM((devices // 2 - 1, *table.shape), jnp.bfloat16),
            pltpu.VMEM(side, jnp.bfloat16),
            pltpu.VMEM(side, jnp.bfloat16),
            pltpu.VMEM((devices, *side), jnp.bfloat16),
            pltpu.VMEM((devices, width, PAIRS), jnp.float32),
            pltpu.VMEM((devices, width, PAIRS), jnp.float32),
            dma((1,)), dma((1,)), dma((1,)), dma((devices // 2 - 1,)),
            dma((devices,)), dma((devices,)), dma((1,)), dma((devices,)), dma((devices,)),
            dma((1,)),
        ],
        compiler_params=pltpu.CompilerParams(collective_id=1, has_side_effects=True),
        name="screen_and_sum",
    )(own_rows, twin_rows, table, lone_at, screened)


def per_device(devices, valence, conduction, screened, blocks, gsphere):
    held_blocks = valence.shape[0] // BLK
    planes = conduction.shape[1]
    twin_points = lax.ppermute(
        gsphere, "grid", [(g, (devices - g) % devices) for g in range(devices)]
    )
    by_plane = jnp.transpose(valence, (1, 0, 2)).reshape(planes, held_blocks, BLK, LANES)
    chosen = spread(blocks, by_plane)
    y_section = densities(
        chosen, jnp.transpose(conduction, (1, 0, 2)), jnp.asarray(z_matrix()), jnp.asarray(y_matrix())
    )
    blocks_y = y_section[:, :, : 2 * KF].reshape(planes, NEG, KF, 2, 2 * PAIRS)
    lowest = jnp.flip(y_section[:, :, 2 * KF :], axis=1)
    lowest = jnp.pad(lowest, ((0, 0), (0, KF - NEG), (0, 0), (0, 0)))
    blocks_y = jnp.concatenate([blocks_y, lowest[:, None]], axis=1).transpose(2, 0, 1, 3, 4)
    moved = exchange(blocks_y, devices)
    moved = moved.transpose(2, 0, 1, 3, 4).reshape(NEG + 1, 2 * GRID_N, 2 * PAIRS)
    qx, qz = gsphere // KF, gsphere % KF
    twin_qx, twin_qz = twin_points // KF, twin_points % KF
    own_at = jnp.where(qz < NEG, qz * ROWS_X + qx, -1)[:, None]
    lone_at = jnp.where(qz < NEG, -1, (qz - NEG) * KF + qx)[:, None]
    twin_at = jnp.where(twin_qz < NEG, -1, (KF - twin_qz) * ROWS_X + KF - twin_qx)[:, None]
    own_rows, twin_rows, table = spheres(moved, jnp.asarray(x_matrix()), own_at, twin_at)
    return tail(own_rows, twin_rows, table, lone_at, screened, devices)[None]


def solution(mesh):
    in_specs = (P("band", "grid", None), P("band", "grid", None), P("grid", None), P(), P("grid"))
    return jax.shard_map(
        functools.partial(per_device, mesh.shape["grid"]), mesh=mesh, in_specs=in_specs,
        out_specs=P("band", "grid", None), check_vma=False,
    )
```

```python
import functools
import math

import jax
import jax.numpy as jnp
import ml_dtypes
import numpy as np
from jax import lax
from jax.experimental import pallas as pl
from jax.experimental.pallas import tpu as pltpu
from jax.sharding import PartitionSpec as P

GRID_N = 96
KF = 32
BLK = 8
PAIRS = 64
SIDE = 4
LANES = GRID_N * GRID_N
PART = LANES // 2
PIECE = PART // SIDE
ROWS_Y = 4
CHUNK = ROWS_Y * GRID_N
NEG = KF // 2 + 1
FULL_X = KF + 1
ROWS_X = 48
MESH = pl.DeviceIdType.MESH


def fourier_parts(length, kept):
    positions = np.arange(length)
    freqs = np.arange(kept) - KF // 2
    phases = (positions[:, None] * freqs[None, :] % length) * (2.0 * math.pi / length)
    factor = 1.0 / math.sqrt(length)
    return np.cos(phases) * factor, np.sin(phases) * factor


def first_table():
    cosine, sine = fourier_parts(GRID_N, KF)
    return np.stack([cosine, -sine], axis=2)


def mixing_table(kept):
    cosine, sine = fourier_parts(GRID_N, kept)
    real_rows = np.stack([cosine, sine], axis=-1)
    imag_rows = np.stack([-sine, cosine], axis=-1)
    return np.stack([real_rows, imag_rows], axis=2)


def z_matrix():
    table = first_table()[:, :NEG]
    out = np.zeros((NEG, ROWS_Y, 2, ROWS_Y, GRID_N))
    for y in range(ROWS_Y):
        out[:, y, :, y, :] = np.transpose(table, (1, 2, 0))
    return out.reshape(NEG * ROWS_Y * 2, CHUNK).astype(ml_dtypes.bfloat16)


def y_matrix():
    table = np.transpose(mixing_table(KF), (1, 2, 0, 3))
    lowest = table[:1] * np.array([1.0, -1.0])
    return np.concatenate([table, lowest]).reshape(2 * KF + 2, 2 * GRID_N).astype(ml_dtypes.bfloat16)


def x_matrix():
    table = np.transpose(mixing_table(FULL_X), (2, 1, 0, 3)).reshape(2, FULL_X, 2 * GRID_N)
    out = np.zeros((2, ROWS_X, 2 * GRID_N))
    out[:, :FULL_X] = table
    return out.reshape(2 * ROWS_X, 2 * GRID_N).astype(ml_dtypes.bfloat16)


def remote(src, dst, send, recv, peer):
    return pltpu.make_async_remote_copy(
        src_ref=src, dst_ref=dst, send_sem=send, recv_sem=recv, device_id=peer, device_id_type=MESH
    )


def greet(peers):
    barrier = pltpu.get_barrier_semaphore()
    for peer in peers:
        pl.semaphore_signal(barrier, inc=1, device_id=peer, device_id_type=MESH)
    pl.semaphore_wait(barrier, len(peers))


def spread_kernel(
    blocks_ref, held_bands, out_ref, src, near0, near1, near2, near3, held, far, mine, full,
    send1, recv1, own1, send2, recv2, send3, recv3, send4, recv4,
):
    band = lax.axis_index("band")
    z, x = band // SIDE, band % SIDE
    near = (near0, near1, near2, near3)

    def along_x(k):
        return {"band": z * SIDE + (x + k) % SIDE}

    def along_z(k):
        return {"band": (z + k) % SIDE * SIDE + x}

    def lanes(q, s):
        return pl.ds(pl.multiple_of(q % 2 * PART + s * PIECE, 128), PIECE)

    count = held_bands.shape[1]
    for b in range(2):
        src[b] = held_bands[:, lax.rem(blocks_ref[b], count)]
    greet([along_x(k) for k in (1, 2, 3)] + [along_z(k) for k in (1, 2, 3)])
    order = (2, 1, 3, 0)
    first = {}
    for j in order:
        s = (z + j) % SIDE
        for k in (2, 1, 3):
            q = (x + k) % SIDE
            copy = remote(
                src.at[q // 2, :, :, lanes(q, s)], near[j].at[x],
                send1.at[j, k - 1], recv1.at[j, k - 1], along_x(k),
            )
            copy.start()
            first[j, k] = copy
        copy = pltpu.make_async_copy(src.at[x // 2, :, :, lanes(x, s)], near[j].at[x], own1.at[j])
        copy.start()
        first[j, 0] = copy
    owner = lax.div(blocks_ref[x // 2], count)
    owner_z, owner_x = owner // SIDE, owner % SIDE
    second = []
    for j in order:
        for k in range(SIDE):
            first[j, k].wait()
        if j == 0:
            far[z] = near[j][owner_x]
        else:
            held[j] = near[j][owner_x]
            copy = remote(
                held.at[j], far.at[z], send2.at[j - 1], recv2.at[j - 1], along_z(j)
            )
            copy.start()
            second.append(copy)
    for copy in second:
        copy.wait()
    picked = far[owner_z]
    mine[...] = picked
    full[x // 2, :, :, lanes(x, z)] = picked
    third = {}
    for k in (2, 1, 3):
        copy = remote(
            mine, full.at[x // 2, :, :, lanes(x, z)], send3.at[k - 1], recv3.at[k - 1], along_z(k)
        )
        copy.start()
        third[k] = copy
    fourth = []
    for j in (0, 1, 3, 2):
        if j:
            third[j].wait()
        s = (z + SIDE - j) % SIDE
        part = full.at[x // 2, :, :, lanes(x, s)]
        for k in (2, 1, 3):
            copy = remote(
                mine if j == 0 else part, part, send4.at[j, k - 1], recv4.at[j, k - 1], along_x(k)
            )
            copy.start()
            fourth.append(copy)
    for copy in fourth:
        copy.wait()
    out_ref[...] = full[...]


def spread(blocks, held_bands):
    planes = held_bands.shape[0]
    whole = (2, planes, BLK, LANES)
    piece = (planes, BLK, PIECE)
    dma = pltpu.SemaphoreType.DMA
    vmem = pl.BlockSpec(memory_space=pltpu.VMEM)
    return pl.pallas_call(
        spread_kernel,
        out_shape=jax.ShapeDtypeStruct(whole, jnp.bfloat16),
        in_specs=[pl.BlockSpec(memory_space=pltpu.SMEM), vmem],
        out_specs=vmem,
        scratch_shapes=[
            pltpu.VMEM(whole, jnp.bfloat16),
            *[pltpu.VMEM((SIDE, *piece), jnp.bfloat16) for _ in range(SIDE)],
            pltpu.VMEM((SIDE, *piece), jnp.bfloat16),
            pltpu.VMEM((SIDE, *piece), jnp.bfloat16),
            pltpu.VMEM(piece, jnp.bfloat16),
            pltpu.VMEM(whole, jnp.bfloat16),
            dma((SIDE, 3)), dma((SIDE, 3)), dma((SIDE,)),
            dma((3,)), dma((3,)), dma((3,)), dma((3,)),
            dma((SIDE, 3)), dma((SIDE, 3)),
        ],
        compiler_params=pltpu.CompilerParams(collective_id=0, has_side_effects=True),
        name="spread_blocks",
    )(blocks, held_bands)


def density_kernel(
    devices, chosen, cond, z_mat, mix, out_ref, sections, made, send, recv, own
):
    me = lax.axis_index("grid")
    half = devices // 2
    ring = half // 2
    z, y, c = me // half, me % half // 2, me % 2
    planes = cond.shape[0]
    barrier = pltpu.get_barrier_semaphore()
    for k in range(1, devices):
        pl.semaphore_signal(
            barrier, inc=1, device_id={"grid": (me + k) % devices}, device_id_type=MESH
        )

    def compute(x):
        def z_step(j, carry):
            both = []
            for part in range(2):
                at = pl.ds(pl.multiple_of((2 * j + part) * CHUNK, 128), CHUNK)
                cc = cond[x, :, at].astype(jnp.float32)
                v = jnp.concatenate(
                    [chosen[0, x, :, at].astype(jnp.float32), chosen[1, x, :, at].astype(jnp.float32)]
                )
                dens = (v[:, None, :] * cc[None, :, :]).reshape(2 * PAIRS, CHUNK)
                summed = lax.dot_general(
                    z_mat[...], dens.astype(jnp.bfloat16), (((1,), (1,)), ((), ())),
                    preferred_element_type=jnp.float32,
                )
                both.append(summed.reshape(NEG, 2 * ROWS_Y, 2 * PAIRS))
            joined = jnp.concatenate(both, axis=1).astype(jnp.bfloat16)
            sections[:, pl.ds(pl.multiple_of(j * 4 * ROWS_Y, 16), 4 * ROWS_Y), :] = joined
            return carry

        lax.fori_loop(0, LANES // CHUNK // 2, z_step, 0)
        made[x, :, NEG] = jnp.zeros((KF, 2, 2 * PAIRS), jnp.bfloat16)

        for q in range(NEG):
            value = jnp.dot(
                mix[...], sections[q], preferred_element_type=jnp.float32
            ).astype(jnp.bfloat16)
            made[x, :, q] = value[: 2 * KF].reshape(KF, 2, 2 * PAIRS)
            made[x, NEG - 1 - q, NEG] = value[2 * KF :]

    def moves(x):
        for dy in sorted(range(ring), key=lambda d: -min(d, ring - d)):
            for dz in (1, 0):
                for dc in (0, 1):
                    k = dz * half + dy * 2 + dc
                    if k:
                        to = (z + dz) % 2 * half + (y + dy) % ring * 2 + (c + dc) % 2
                        source = (z + dz) % 2 * half + (y + ring - dy) % ring * 2 + (c + dc) % 2
                        yield k, to, source

    def post(x):
        for k, to, _ in moves(x):
            remote(
                made.at[x, to], out_ref.at[me, x], send.at[x, k], recv.at[x, k], {"grid": to}
            ).start()
        pltpu.make_async_copy(made.at[x, me], out_ref.at[me, x], own.at[x]).start()

    compute(0)
    pl.semaphore_wait(barrier, devices - 1)
    post(0)

    def plane(x, carry):
        compute(x)
        post(x)
        return carry

    lax.fori_loop(1, planes, plane, 0)

    def finish(x, carry):
        for k, to, source in moves(x):
            remote(
                made.at[x, to], out_ref.at[source, x], send.at[x, k], recv.at[x, k], {"grid": to}
            ).wait()
        pltpu.make_async_copy(made.at[x, me], out_ref.at[me, x], own.at[x]).wait()
        return carry

    lax.fori_loop(0, planes, finish, 0)


def densities(chosen, cond, z_mat, mix, devices):
    planes = cond.shape[0]
    dma = pltpu.SemaphoreType.DMA
    vmem = pl.BlockSpec(memory_space=pltpu.VMEM)
    return pl.pallas_call(
        functools.partial(density_kernel, devices),
        out_shape=jax.ShapeDtypeStruct((devices, planes, NEG + 1, 2, 2 * PAIRS), jnp.bfloat16),
        in_specs=[vmem] * 4,
        out_specs=pl.BlockSpec(memory_space=pl.ANY),
        scratch_shapes=[
            pltpu.VMEM((NEG, 2 * GRID_N, 2 * PAIRS), jnp.bfloat16),
            pltpu.VMEM((planes, devices, NEG + 1, 2, 2 * PAIRS), jnp.bfloat16),
            dma((planes, devices)), dma((planes, devices)), dma((planes,)),
        ],
        compiler_params=pltpu.CompilerParams(collective_id=2, has_side_effects=True),
        name="density_and_exchange",
    )(chosen, cond, z_mat, mix)


def one_hot(index, count):
    rows = lax.broadcasted_iota(jnp.int32, (count, index.shape[1]), 0)
    return jnp.where(rows == index, 1.0, 0.0).astype(jnp.bfloat16)


def pick(index, table):
    return lax.dot_general(
        one_hot(index, table.shape[0]), table, (((0,), (0,)), ((), ())),
        preferred_element_type=jnp.float32,
    )


def sphere_kernel(moved, mix, own_at, twin_at, own_ref, twin_ref, table_ref, table):
    for q in range(NEG + 1):
        part = jnp.dot(mix[...], moved[q], preferred_element_type=jnp.float32)
        both = jnp.concatenate([part[:ROWS_X], part[ROWS_X:]], axis=1).astype(jnp.bfloat16)
        if q < NEG:
            table[q * ROWS_X : (q + 1) * ROWS_X] = both
        else:
            table_ref[...] = both[:KF]
    own_ref[...] = pick(own_at[...], table[...]).astype(jnp.bfloat16)
    twin = pick(twin_at[...], table[...])
    lanes = lax.broadcasted_iota(jnp.int32, twin.shape, 1)
    twin_ref[...] = jnp.where(lanes < 2 * PAIRS, twin, -twin).astype(jnp.bfloat16)


def spheres(moved, mix, own_at, twin_at):
    rows = jax.ShapeDtypeStruct((own_at.shape[1], 4 * PAIRS), jnp.bfloat16)
    vmem = pl.BlockSpec(memory_space=pltpu.VMEM)
    return pl.pallas_call(
        sphere_kernel,
        out_shape=[rows, rows, jax.ShapeDtypeStruct((KF, 4 * PAIRS), jnp.bfloat16)],
        in_specs=[vmem] * 4,
        out_specs=[vmem] * 3,
        scratch_shapes=[pltpu.VMEM((NEG * ROWS_X, 4 * PAIRS), jnp.bfloat16)],
        name="x_and_sphere",
    )(moved, mix, own_at, twin_at)


def tail_kernel(
    devices, own_rows, twin_rows, table, lone_at, screened, out_ref,
    weights, total, got, tables, side_a, side_b, rows, parts, arrived,
    swap_send, swap_recv, lone_send, lone_recv, send, recv, own, sum_send, sum_recv, fetched,
):
    fetch = pltpu.make_async_copy(screened, weights, fetched.at[0])
    fetch.start()
    me = lax.axis_index("grid")
    half = devices // 2
    ring = half // 2
    z, y, c = me // half, me % half // 2, me % 2

    def at(zz, yy, cc):
        return zz * half + yy % ring * 2 + cc

    greet([{"grid": (me + k) % devices} for k in range(1, devices)])
    paired = (me != 0) & (me != half)
    swap = remote(
        twin_rows, got, swap_send.at[0], swap_recv.at[0], {"grid": (devices - me) % devices}
    )
    helper = (me > 0) & (me < half)

    @pl.when(helper)
    def _():
        remote(
            table, tables.at[me - 1], lone_send.at[0], lone_recv.at[me - 1], {"grid": 0}
        ).start()

    @pl.when(paired)
    def _():
        swap.start()
        swap.wait()

    @pl.when(me == half)
    def _():
        got[...] = twin_rows[...]

    @pl.when(me == 0)
    def _():
        for i in range(half - 1):
            remote(
                table, tables.at[i], lone_send.at[0], lone_recv.at[i], {"grid": i + 1}
            ).wait_recv()
        count = (half - 1) * KF
        picked = pick(lone_at[...], tables[...].reshape(count, 4 * PAIRS))
        got[...] = picked.astype(jnp.bfloat16)

    @pl.when(helper)
    def _():
        remote(
            table, tables.at[me - 1], lone_send.at[0], lone_recv.at[me - 1], {"grid": 0}
        ).wait_send()

    sphere = own_rows[...].astype(jnp.float32) + got[...].astype(jnp.float32)
    real, imag = sphere[:, : 2 * PAIRS], sphere[:, 2 * PAIRS :]
    side_b[...] = jnp.concatenate([real[:, PAIRS:], imag[:, PAIRS:]], axis=1).astype(jnp.bfloat16)
    side_a[...] = jnp.concatenate([real[:, :PAIRS], imag[:, :PAIRS]], axis=1).astype(jnp.bfloat16)
    local = pltpu.make_async_copy(side_b, rows.at[me], own.at[0])
    local.start()
    started = []

    def push(slot, peer, from_input=False):
        copy = remote(
            side_b if from_input else rows.at[slot], rows.at[slot],
            send.at[len(started)], recv.at[slot], {"grid": peer},
        )
        copy.start()
        started.append(copy)

    def landed(slot):
        pltpu.make_async_remote_copy(
            src_ref=rows.at[slot], dst_ref=rows.at[slot], send_sem=own.at[0],
            recv_sem=recv.at[slot], device_id={"grid": at(z, y, 1 - c)}, device_id_type=MESH,
        ).wait_recv()

    up, down, twin = at(z, y + 1, c), at(z, y + ring - 1, c), at(z, y, 1 - c)
    push(me, at(1 - z, y, c), True)
    push(me, up, True)
    push(me, down, True)
    push(me, twin, True)
    other = at(1 - z, y, c)
    landed(other)
    push(other, up)
    push(other, down)
    push(other, twin)
    count = side_a.shape[0]
    total[...] = jnp.zeros_like(total)
    local.wait()
    fetch.wait()

    def screen(zz, back):
        landed(at(zz, y + back, 1 - c))
        first = at(zz, y + back, 0)
        columns = pl.ds(pl.multiple_of(first * count, 128), 2 * count)
        pair = rows[pl.ds(first, 2)].reshape(2 * count, 2 * PAIRS)
        total[...] += jnp.dot(weights[:, columns], pair, preferred_element_type=jnp.float32)

    ready = [(z, 0), (1 - z, 0)]
    for t in range(1, ring // 2 + 1):
        fresh = []
        for zz, ups in ((z, ring // 2), (1 - z, ring // 2 - 1)):
            for steps, back, peer in ((ups, ring - t, up), (ring - 1 - ups, t, down)):
                if t <= steps:
                    slot = at(zz, y + back, c)
                    landed(slot)
                    if t < steps:
                        push(slot, peer)
                    push(slot, twin)
                    fresh.append((zz, back))
        for pair in ready:
            screen(*pair)
        ready = fresh
    for pair in ready:
        screen(*pair)
    product = lax.dot_general(
        side_a[...], total[...].astype(jnp.bfloat16), (((0,), (0,)), ((), ())), preferred_element_type=jnp.float32
    )
    value = product[:PAIRS, :PAIRS] + product[PAIRS:, PAIRS:]
    width = PAIRS // devices
    for g in range(devices):
        parts[g] = value[g * width : (g + 1) * width]
    for copy in started:
        copy.wait_send()
    moves = []
    for k in range(1, devices):
        peer = (me + k) % devices
        copy = remote(
            parts.at[peer], arrived.at[k], sum_send.at[k], sum_recv.at[k], {"grid": peer}
        )
        copy.start()
        moves.append(copy)
    result = parts[me]
    for copy in moves:
        copy.wait()
    for k in range(1, devices):
        result = result + arrived[k]
    out_ref[...] = result


def tail(own_rows, twin_rows, table, lone_at, screened, devices):
    vmem = pl.BlockSpec(memory_space=pltpu.VMEM)
    dma = pltpu.SemaphoreType.DMA
    width = PAIRS // devices
    side = (own_rows.shape[0], 2 * PAIRS)
    return pl.pallas_call(
        functools.partial(tail_kernel, devices),
        out_shape=jax.ShapeDtypeStruct((width, PAIRS), jnp.float32),
        in_specs=[vmem] * 4 + [pl.BlockSpec(memory_space=pl.ANY)],
        out_specs=vmem,
        scratch_shapes=[
            pltpu.VMEM(screened.shape, jnp.bfloat16),
            pltpu.VMEM(side, jnp.float32),
            pltpu.VMEM(own_rows.shape, jnp.bfloat16),
            pltpu.VMEM((devices // 2 - 1, *table.shape), jnp.bfloat16),
            pltpu.VMEM(side, jnp.bfloat16),
            pltpu.VMEM(side, jnp.bfloat16),
            pltpu.VMEM((devices, *side), jnp.bfloat16),
            pltpu.VMEM((devices, width, PAIRS), jnp.float32),
            pltpu.VMEM((devices, width, PAIRS), jnp.float32),
            dma((1,)), dma((1,)), dma((1,)), dma((devices // 2 - 1,)),
            dma((devices,)), dma((devices,)), dma((1,)), dma((devices,)), dma((devices,)),
            dma((1,)),
        ],
        compiler_params=pltpu.CompilerParams(collective_id=1, has_side_effects=True),
        name="screen_and_sum",
    )(own_rows, twin_rows, table, lone_at, screened)


def per_device(devices, valence, conduction, screened, blocks, gsphere):
    held_blocks = valence.shape[0] // BLK
    planes = conduction.shape[1]
    twin_points = lax.ppermute(
        gsphere, "grid", [(g, (devices - g) % devices) for g in range(devices)]
    )
    by_plane = jnp.transpose(valence, (1, 0, 2)).reshape(planes, held_blocks, BLK, LANES)
    chosen = spread(blocks, by_plane)
    moved = densities(
        chosen, jnp.transpose(conduction, (1, 0, 2)), jnp.asarray(z_matrix()),
        jnp.asarray(y_matrix()), devices,
    )
    moved = moved.transpose(2, 0, 1, 3, 4).reshape(NEG + 1, 2 * GRID_N, 2 * PAIRS)
    qx, qz = gsphere // KF, gsphere % KF
    twin_qx, twin_qz = twin_points // KF, twin_points % KF
    own_at = jnp.where(qz < NEG, qz * ROWS_X + qx, -1)[None]
    lone_at = jnp.where(qz < NEG, -1, (qz - NEG) * KF + qx)[None]
    twin_at = jnp.where(twin_qz < NEG, -1, (KF - twin_qz) * ROWS_X + KF - twin_qx)[None]
    own_rows, twin_rows, table = spheres(moved, jnp.asarray(x_matrix()), own_at, twin_at)
    return tail(own_rows, twin_rows, table, lone_at, screened, devices)[None]


def solution(mesh):
    in_specs = (P("band", "grid", None), P("band", "grid", None), P("grid", None), P(), P("grid"))
    return jax.shard_map(
        functools.partial(per_device, mesh.shape["grid"]), mesh=mesh, in_specs=in_specs,
        out_specs=P("band", "grid", None), check_vma=False,
    )
```

```python
import functools
import math

import jax
import jax.numpy as jnp
import ml_dtypes
import numpy as np
from jax import lax
from jax.experimental import pallas as pl
from jax.experimental.pallas import tpu as pltpu
from jax.sharding import PartitionSpec as P

GRID_N = 96
KF = 32
BLK = 8
PAIRS = 64
SIDE = 4
LANES = GRID_N * GRID_N
PART = LANES // 2
PIECE = PART // SIDE
ROWS_Y = 4
CHUNK = ROWS_Y * GRID_N
NEG = KF // 2 + 1
FULL_X = KF + 1
ROWS_X = 48
MESH = pl.DeviceIdType.MESH


def fourier_parts(length, kept):
    positions = np.arange(length)
    freqs = np.arange(kept) - KF // 2
    phases = (positions[:, None] * freqs[None, :] % length) * (2.0 * math.pi / length)
    factor = 1.0 / math.sqrt(length)
    return np.cos(phases) * factor, np.sin(phases) * factor


def first_table():
    cosine, sine = fourier_parts(GRID_N, KF)
    return np.stack([cosine, -sine], axis=2)


def mixing_table(kept):
    cosine, sine = fourier_parts(GRID_N, kept)
    real_rows = np.stack([cosine, sine], axis=-1)
    imag_rows = np.stack([-sine, cosine], axis=-1)
    return np.stack([real_rows, imag_rows], axis=2)


def z_matrix():
    table = first_table()[:, :NEG]
    out = np.zeros((NEG, ROWS_Y, 2, ROWS_Y, GRID_N))
    for y in range(ROWS_Y):
        out[:, y, :, y, :] = np.transpose(table, (1, 2, 0))
    return out.reshape(NEG * ROWS_Y * 2, CHUNK).astype(ml_dtypes.bfloat16)


def y_matrix():
    table = np.transpose(mixing_table(KF), (1, 2, 0, 3))
    lowest = table[:1] * np.array([1.0, -1.0])
    return np.concatenate([table, lowest]).reshape(2 * KF + 2, 2 * GRID_N).astype(ml_dtypes.bfloat16)


def x_matrix():
    table = np.transpose(mixing_table(FULL_X), (2, 1, 0, 3)).reshape(2, FULL_X, 2 * GRID_N)
    out = np.zeros((2, ROWS_X, 2 * GRID_N))
    out[:, :FULL_X] = table
    return out.reshape(2 * ROWS_X, 2 * GRID_N).astype(ml_dtypes.bfloat16)


def remote(src, dst, send, recv, peer):
    return pltpu.make_async_remote_copy(
        src_ref=src, dst_ref=dst, send_sem=send, recv_sem=recv, device_id=peer, device_id_type=MESH
    )


def greet(peers):
    barrier = pltpu.get_barrier_semaphore()
    for peer in peers:
        pl.semaphore_signal(barrier, inc=1, device_id=peer, device_id_type=MESH)
    pl.semaphore_wait(barrier, len(peers))


def spread_kernel(
    blocks_ref, held_bands, out_ref, src, near0, near1, near2, near3, held, far, mine, full,
    send1, recv1, own1, send2, recv2, send3, recv3, send4, recv4,
):
    band = lax.axis_index("band")
    z, x = band // SIDE, band % SIDE
    near = (near0, near1, near2, near3)

    def along_x(k):
        return {"band": z * SIDE + (x + k) % SIDE}

    def along_z(k):
        return {"band": (z + k) % SIDE * SIDE + x}

    def lanes(q, s):
        return pl.ds(pl.multiple_of(q % 2 * PART + s * PIECE, 128), PIECE)

    count = held_bands.shape[1]
    for b in range(2):
        src[b] = held_bands[:, lax.rem(blocks_ref[b], count)]
    greet([along_x(k) for k in (1, 2, 3)] + [along_z(k) for k in (1, 2, 3)])
    order = (2, 1, 3, 0)
    first = {}
    for j in order:
        s = (z + j) % SIDE
        for k in (2, 1, 3):
            q = (x + k) % SIDE
            copy = remote(
                src.at[q // 2, :, :, lanes(q, s)], near[j].at[x],
                send1.at[j, k - 1], recv1.at[j, k - 1], along_x(k),
            )
            copy.start()
            first[j, k] = copy
        copy = pltpu.make_async_copy(src.at[x // 2, :, :, lanes(x, s)], near[j].at[x], own1.at[j])
        copy.start()
        first[j, 0] = copy
    owner = lax.div(blocks_ref[x // 2], count)
    owner_z, owner_x = owner // SIDE, owner % SIDE
    second = []
    for j in order:
        for k in range(SIDE):
            first[j, k].wait()
        if j == 0:
            far[z] = near[j][owner_x]
        else:
            held[j] = near[j][owner_x]
            copy = remote(
                held.at[j], far.at[z], send2.at[j - 1], recv2.at[j - 1], along_z(j)
            )
            copy.start()
            second.append(copy)
    for copy in second:
        copy.wait()
    picked = far[owner_z]
    mine[...] = picked
    full[x // 2, :, :, lanes(x, z)] = picked
    third = {}
    for k in (2, 1, 3):
        copy = remote(
            mine, full.at[x // 2, :, :, lanes(x, z)], send3.at[k - 1], recv3.at[k - 1], along_z(k)
        )
        copy.start()
        third[k] = copy
    fourth = []
    for j in (0, 1, 3, 2):
        if j:
            third[j].wait()
        s = (z + SIDE - j) % SIDE
        part = full.at[x // 2, :, :, lanes(x, s)]
        for k in (2, 1, 3):
            copy = remote(
                mine if j == 0 else part, part, send4.at[j, k - 1], recv4.at[j, k - 1], along_x(k)
            )
            copy.start()
            fourth.append(copy)
    for copy in fourth:
        copy.wait()
    out_ref[...] = full[...]


def spread(blocks, held_bands):
    planes = held_bands.shape[0]
    whole = (2, planes, BLK, LANES)
    piece = (planes, BLK, PIECE)
    dma = pltpu.SemaphoreType.DMA
    vmem = pl.BlockSpec(memory_space=pltpu.VMEM)
    return pl.pallas_call(
        spread_kernel,
        out_shape=jax.ShapeDtypeStruct(whole, jnp.bfloat16),
        in_specs=[pl.BlockSpec(memory_space=pltpu.SMEM), vmem],
        out_specs=vmem,
        scratch_shapes=[
            pltpu.VMEM(whole, jnp.bfloat16),
            *[pltpu.VMEM((SIDE, *piece), jnp.bfloat16) for _ in range(SIDE)],
            pltpu.VMEM((SIDE, *piece), jnp.bfloat16),
            pltpu.VMEM((SIDE, *piece), jnp.bfloat16),
            pltpu.VMEM(piece, jnp.bfloat16),
            pltpu.VMEM(whole, jnp.bfloat16),
            dma((SIDE, 3)), dma((SIDE, 3)), dma((SIDE,)),
            dma((3,)), dma((3,)), dma((3,)), dma((3,)),
            dma((SIDE, 3)), dma((SIDE, 3)),
        ],
        compiler_params=pltpu.CompilerParams(collective_id=0, has_side_effects=True),
        name="spread_blocks",
    )(blocks, held_bands)


def density_kernel(
    devices, chosen, cond, z_mat, mix, points, out_ref, twin_points, sections, made,
    send, recv, own, point_send, point_recv,
):
    me = lax.axis_index("grid")
    half = devices // 2
    ring = half // 2
    z, y, c = me // half, me % half // 2, me % 2
    planes = cond.shape[0]
    barrier = pltpu.get_barrier_semaphore()
    for k in range(1, devices):
        pl.semaphore_signal(
            barrier, inc=1, device_id={"grid": (me + k) % devices}, device_id_type=MESH
        )

    def compute(x):
        def z_step(j, carry):
            both = []
            for part in range(2):
                at = pl.ds(pl.multiple_of((2 * j + part) * CHUNK, 128), CHUNK)
                cc = cond[x, :, at].astype(jnp.float32)
                v = jnp.concatenate(
                    [chosen[0, x, :, at].astype(jnp.float32), chosen[1, x, :, at].astype(jnp.float32)]
                )
                dens = (v[:, None, :] * cc[None, :, :]).reshape(2 * PAIRS, CHUNK)
                summed = lax.dot_general(
                    z_mat[...], dens.astype(jnp.bfloat16), (((1,), (1,)), ((), ())),
                    preferred_element_type=jnp.float32,
                )
                both.append(summed.reshape(NEG, 2 * ROWS_Y, 2 * PAIRS))
            joined = jnp.concatenate(both, axis=1).astype(jnp.bfloat16)
            sections[:, pl.ds(pl.multiple_of(j * 4 * ROWS_Y, 16), 4 * ROWS_Y), :] = joined
            return carry

        lax.fori_loop(0, LANES // CHUNK // 2, z_step, 0)
        made[x, :, NEG] = jnp.zeros((KF, 2, 2 * PAIRS), jnp.bfloat16)

        for q in range(NEG):
            value = jnp.dot(
                mix[...], sections[q], preferred_element_type=jnp.float32
            ).astype(jnp.bfloat16)
            made[x, :, q] = value[: 2 * KF].reshape(KF, 2, 2 * PAIRS)
            made[x, NEG - 1 - q, NEG] = value[2 * KF :]

    def moves(x):
        for dy in sorted(range(ring), key=lambda d: -min(d, ring - d)):
            for dz in (1, 0):
                for dc in (0, 1):
                    k = dz * half + dy * 2 + dc
                    if k:
                        to = (z + dz) % 2 * half + (y + dy) % ring * 2 + (c + dc) % 2
                        source = (z + dz) % 2 * half + (y + ring - dy) % ring * 2 + (c + dc) % 2
                        yield k, to, source

    def post(x):
        for k, to, _ in moves(x):
            remote(
                made.at[x, to], out_ref.at[me, x], send.at[x, k], recv.at[x, k], {"grid": to}
            ).start()
        pltpu.make_async_copy(made.at[x, me], out_ref.at[me, x], own.at[x]).start()

    compute(0)
    pl.semaphore_wait(barrier, devices - 1)
    post(0)
    paired = (me != 0) & (me != half)
    swap = remote(
        points, twin_points, point_send.at[0], point_recv.at[0], {"grid": (devices - me) % devices}
    )
    keep = pltpu.make_async_copy(points, twin_points, point_send.at[0])

    @pl.when(paired)
    def _():
        swap.start()

    @pl.when(jnp.logical_not(paired))
    def _():
        keep.start()
        keep.wait()

    def plane(x, carry):
        compute(x)
        post(x)
        return carry

    lax.fori_loop(1, planes, plane, 0)

    def finish(x, carry):
        for k, to, source in moves(x):
            remote(
                made.at[x, to], out_ref.at[source, x], send.at[x, k], recv.at[x, k], {"grid": to}
            ).wait()
        pltpu.make_async_copy(made.at[x, me], out_ref.at[me, x], own.at[x]).wait()
        return carry

    lax.fori_loop(0, planes, finish, 0)

    @pl.when(paired)
    def _():
        swap.wait()


def densities(chosen, cond, z_mat, mix, points, devices):
    planes = cond.shape[0]
    dma = pltpu.SemaphoreType.DMA
    vmem = pl.BlockSpec(memory_space=pltpu.VMEM)
    anywhere = pl.BlockSpec(memory_space=pl.ANY)
    return pl.pallas_call(
        functools.partial(density_kernel, devices),
        out_shape=[
            jax.ShapeDtypeStruct((devices, planes, NEG + 1, 2, 2 * PAIRS), jnp.bfloat16),
            jax.ShapeDtypeStruct(points.shape, points.dtype),
        ],
        in_specs=[vmem] * 4 + [anywhere],
        out_specs=[anywhere] * 2,
        scratch_shapes=[
            pltpu.VMEM((NEG, 2 * GRID_N, 2 * PAIRS), jnp.bfloat16),
            pltpu.VMEM((planes, devices, NEG + 1, 2, 2 * PAIRS), jnp.bfloat16),
            dma((planes, devices)), dma((planes, devices)), dma((planes,)), dma((1,)), dma((1,)),
        ],
        compiler_params=pltpu.CompilerParams(collective_id=2, has_side_effects=True),
        name="density_and_exchange",
    )(chosen, cond, z_mat, mix, points)


def one_hot(index, count):
    rows = lax.broadcasted_iota(jnp.int32, (count, index.shape[1]), 0)
    return jnp.where(rows == index, 1.0, 0.0).astype(jnp.bfloat16)


def pick(index, table):
    return lax.dot_general(
        one_hot(index, table.shape[0]), table, (((0,), (0,)), ((), ())),
        preferred_element_type=jnp.float32,
    )


def sphere_rows(moved, mix, points, twin_points, own_rows, twin_rows, table_ref, table):
    for q in range(NEG + 1):
        rows = moved[:, :, q].reshape(2 * GRID_N, 2 * PAIRS)
        part = jnp.dot(mix[...], rows, preferred_element_type=jnp.float32)
        both = jnp.concatenate([part[:ROWS_X], part[ROWS_X:]], axis=1).astype(jnp.bfloat16)
        if q < NEG:
            table[q * ROWS_X : (q + 1) * ROWS_X] = both
        else:
            table_ref[...] = both[:KF]
    qx, qz = lax.div(points, KF), lax.rem(points, KF)
    twin_qx, twin_qz = lax.div(twin_points, KF), lax.rem(twin_points, KF)
    own_at = jnp.where(qz < NEG, qz * ROWS_X + qx, -1)
    twin_at = jnp.where(twin_qz < NEG, -1, (KF - twin_qz) * ROWS_X + KF - twin_qx)
    own_rows[...] = pick(own_at, table[...]).astype(jnp.bfloat16)
    twin = pick(twin_at, table[...])
    lanes = lax.broadcasted_iota(jnp.int32, twin.shape, 1)
    twin_rows[...] = jnp.where(lanes < 2 * PAIRS, twin, -twin).astype(jnp.bfloat16)
    return jnp.where(qz < NEG, -1, (qz - NEG) * KF + qx)


def tail_kernel(
    devices, moved, mix, points, twin_points, screened, out_ref,
    own_rows, twin_rows, table, found, weights, total, got, tables, side_a, side_b, rows, parts, arrived,
    swap_send, swap_recv, lone_send, lone_recv, send, recv, own, sum_send, sum_recv, fetched,
):
    fetch = pltpu.make_async_copy(screened, weights, fetched.at[0])
    fetch.start()
    me = lax.axis_index("grid")
    half = devices // 2
    ring = half // 2
    z, y, c = me // half, me % half // 2, me % 2

    def at(zz, yy, cc):
        return zz * half + yy % ring * 2 + cc

    barrier = pltpu.get_barrier_semaphore()
    for k in range(1, devices):
        pl.semaphore_signal(
            barrier, inc=1, device_id={"grid": (me + k) % devices}, device_id_type=MESH
        )
    lone_at = sphere_rows(
        moved, mix, points[...], twin_points[...], own_rows, twin_rows, table, found
    )
    pl.semaphore_wait(barrier, devices - 1)
    paired = (me != 0) & (me != half)
    swap = remote(
        twin_rows, got, swap_send.at[0], swap_recv.at[0], {"grid": (devices - me) % devices}
    )
    helper = (me > 0) & (me < half)

    @pl.when(helper)
    def _():
        remote(
            table, tables.at[me - 1], lone_send.at[0], lone_recv.at[me - 1], {"grid": 0}
        ).start()

    @pl.when(paired)
    def _():
        swap.start()
        swap.wait()

    @pl.when(me == half)
    def _():
        got[...] = twin_rows[...]

    @pl.when(me == 0)
    def _():
        for i in range(half - 1):
            remote(
                table, tables.at[i], lone_send.at[0], lone_recv.at[i], {"grid": i + 1}
            ).wait_recv()
        count = (half - 1) * KF
        picked = pick(lone_at, tables[...].reshape(count, 4 * PAIRS))
        got[...] = picked.astype(jnp.bfloat16)

    @pl.when(helper)
    def _():
        remote(
            table, tables.at[me - 1], lone_send.at[0], lone_recv.at[me - 1], {"grid": 0}
        ).wait_send()

    sphere = own_rows[...].astype(jnp.float32) + got[...].astype(jnp.float32)
    real, imag = sphere[:, : 2 * PAIRS], sphere[:, 2 * PAIRS :]
    side_b[...] = jnp.concatenate([real[:, PAIRS:], imag[:, PAIRS:]], axis=1).astype(jnp.bfloat16)
    side_a[...] = jnp.concatenate([real[:, :PAIRS], imag[:, :PAIRS]], axis=1).astype(jnp.bfloat16)
    local = pltpu.make_async_copy(side_b, rows.at[me], own.at[0])
    local.start()
    started = []

    def push(slot, peer, from_input=False):
        copy = remote(
            side_b if from_input else rows.at[slot], rows.at[slot],
            send.at[len(started)], recv.at[slot], {"grid": peer},
        )
        copy.start()
        started.append(copy)

    def landed(slot):
        pltpu.make_async_remote_copy(
            src_ref=rows.at[slot], dst_ref=rows.at[slot], send_sem=own.at[0],
            recv_sem=recv.at[slot], device_id={"grid": at(z, y, 1 - c)}, device_id_type=MESH,
        ).wait_recv()

    up, down, twin = at(z, y + 1, c), at(z, y + ring - 1, c), at(z, y, 1 - c)
    push(me, at(1 - z, y, c), True)
    push(me, up, True)
    push(me, down, True)
    push(me, twin, True)
    other = at(1 - z, y, c)
    landed(other)
    push(other, up)
    push(other, down)
    push(other, twin)
    count = side_a.shape[0]
    total[...] = jnp.zeros_like(total)
    local.wait()
    fetch.wait()

    def screen(zz, back):
        landed(at(zz, y + back, 1 - c))
        first = at(zz, y + back, 0)
        columns = pl.ds(pl.multiple_of(first * count, 128), 2 * count)
        pair = rows[pl.ds(first, 2)].reshape(2 * count, 2 * PAIRS)
        total[...] += jnp.dot(weights[:, columns], pair, preferred_element_type=jnp.float32)

    ready = [(z, 0), (1 - z, 0)]
    for t in range(1, ring // 2 + 1):
        fresh = []
        for zz, ups in ((z, ring // 2), (1 - z, ring // 2 - 1)):
            for steps, back, peer in ((ups, ring - t, up), (ring - 1 - ups, t, down)):
                if t <= steps:
                    slot = at(zz, y + back, c)
                    landed(slot)
                    if t < steps:
                        push(slot, peer)
                    push(slot, twin)
                    fresh.append((zz, back))
        for pair in ready:
            screen(*pair)
        ready = fresh
    for pair in ready:
        screen(*pair)
    product = lax.dot_general(
        side_a[...], total[...].astype(jnp.bfloat16), (((0,), (0,)), ((), ())), preferred_element_type=jnp.float32
    )
    value = product[:PAIRS, :PAIRS] + product[PAIRS:, PAIRS:]
    width = PAIRS // devices
    for g in range(devices):
        parts[g] = value[g * width : (g + 1) * width]
    for copy in started:
        copy.wait_send()
    moves = []
    for k in range(1, devices):
        peer = (me + k) % devices
        copy = remote(
            parts.at[peer], arrived.at[k], sum_send.at[k], sum_recv.at[k], {"grid": peer}
        )
        copy.start()
        moves.append(copy)
    result = parts[me]
    for copy in moves:
        copy.wait()
    for k in range(1, devices):
        result = result + arrived[k]
    out_ref[...] = result


def tail(moved, mix, points, twin_points, screened, devices):
    vmem = pl.BlockSpec(memory_space=pltpu.VMEM)
    dma = pltpu.SemaphoreType.DMA
    width = PAIRS // devices
    side = (points.shape[1], 2 * PAIRS)
    both = (points.shape[1], 4 * PAIRS)
    table = (KF, 4 * PAIRS)
    return pl.pallas_call(
        functools.partial(tail_kernel, devices),
        out_shape=jax.ShapeDtypeStruct((width, PAIRS), jnp.float32),
        in_specs=[vmem] * 4 + [pl.BlockSpec(memory_space=pl.ANY)],
        out_specs=vmem,
        scratch_shapes=[
            pltpu.VMEM(both, jnp.bfloat16),
            pltpu.VMEM(both, jnp.bfloat16),
            pltpu.VMEM(table, jnp.bfloat16),
            pltpu.VMEM((NEG * ROWS_X, 4 * PAIRS), jnp.bfloat16),
            pltpu.VMEM(screened.shape, jnp.bfloat16),
            pltpu.VMEM(side, jnp.float32),
            pltpu.VMEM(both, jnp.bfloat16),
            pltpu.VMEM((devices // 2 - 1, *table), jnp.bfloat16),
            pltpu.VMEM(side, jnp.bfloat16),
            pltpu.VMEM(side, jnp.bfloat16),
            pltpu.VMEM((devices, *side), jnp.bfloat16),
            pltpu.VMEM((devices, width, PAIRS), jnp.float32),
            pltpu.VMEM((devices, width, PAIRS), jnp.float32),
            dma((1,)), dma((1,)), dma((1,)), dma((devices // 2 - 1,)),
            dma((devices,)), dma((devices,)), dma((1,)), dma((devices,)), dma((devices,)),
            dma((1,)),
        ],
        compiler_params=pltpu.CompilerParams(collective_id=1, has_side_effects=True),
        name="screen_and_sum",
    )(moved, mix, points, twin_points, screened)


def per_device(devices, valence, conduction, screened, blocks, gsphere):
    held_blocks = valence.shape[0] // BLK
    planes = conduction.shape[1]
    by_plane = jnp.transpose(valence, (1, 0, 2)).reshape(planes, held_blocks, BLK, LANES)
    chosen = spread(blocks, by_plane)
    points = gsphere[None]
    moved, twin_points = densities(
        chosen, jnp.transpose(conduction, (1, 0, 2)), jnp.asarray(z_matrix()),
        jnp.asarray(y_matrix()), points, devices,
    )
    return tail(moved, jnp.asarray(x_matrix()), points, twin_points, screened, devices)[None]


def solution(mesh):
    in_specs = (P("band", "grid", None), P("band", "grid", None), P("grid", None), P(), P("grid"))
    return jax.shard_map(
        functools.partial(per_device, mesh.shape["grid"]), mesh=mesh, in_specs=in_specs,
        out_specs=P("band", "grid", None), check_vma=False,
    )
```

```python
import functools
import math

import jax
import jax.numpy as jnp
import ml_dtypes
import numpy as np
from jax import lax
from jax.experimental import pallas as pl
from jax.experimental.pallas import tpu as pltpu
from jax.sharding import PartitionSpec as P

GRID_N = 96
KF = 32
BLK = 8
PAIRS = 64
SIDE = 4
LANES = GRID_N * GRID_N
PART = LANES // 2
PIECE = PART // SIDE
ROWS_Y = 4
CHUNK = ROWS_Y * GRID_N
NEG = KF // 2 + 1
FULL_X = KF + 1
ROWS_X = 48
MESH = pl.DeviceIdType.MESH


def fourier_parts(length, kept):
    positions = np.arange(length)
    freqs = np.arange(kept) - KF // 2
    phases = (positions[:, None] * freqs[None, :] % length) * (2.0 * math.pi / length)
    factor = 1.0 / math.sqrt(length)
    return np.cos(phases) * factor, np.sin(phases) * factor


def first_table():
    cosine, sine = fourier_parts(GRID_N, KF)
    return np.stack([cosine, -sine], axis=2)


def mixing_table(kept):
    cosine, sine = fourier_parts(GRID_N, kept)
    real_rows = np.stack([cosine, sine], axis=-1)
    imag_rows = np.stack([-sine, cosine], axis=-1)
    return np.stack([real_rows, imag_rows], axis=2)


def z_matrix():
    table = first_table()[:, :NEG]
    out = np.zeros((NEG, ROWS_Y, 2, ROWS_Y, GRID_N))
    for y in range(ROWS_Y):
        out[:, y, :, y, :] = np.transpose(table, (1, 2, 0))
    return out.reshape(NEG * ROWS_Y * 2, CHUNK).astype(ml_dtypes.bfloat16)


def y_matrix():
    table = np.transpose(mixing_table(KF), (1, 2, 0, 3))
    lowest = table[:1] * np.array([1.0, -1.0])
    return np.concatenate([table, lowest]).reshape(2 * KF + 2, 2 * GRID_N).astype(ml_dtypes.bfloat16)


def x_matrix():
    table = np.transpose(mixing_table(FULL_X), (2, 1, 0, 3)).reshape(2, FULL_X, 2 * GRID_N)
    out = np.zeros((2, ROWS_X, 2 * GRID_N))
    out[:, :FULL_X] = table
    return out.reshape(2 * ROWS_X, 2 * GRID_N).astype(ml_dtypes.bfloat16)


def remote(src, dst, send, recv, peer):
    return pltpu.make_async_remote_copy(
        src_ref=src, dst_ref=dst, send_sem=send, recv_sem=recv, device_id=peer, device_id_type=MESH
    )


def greet(peers):
    barrier = pltpu.get_barrier_semaphore()
    for peer in peers:
        pl.semaphore_signal(barrier, inc=1, device_id=peer, device_id_type=MESH)
    pl.semaphore_wait(barrier, len(peers))


def spread_kernel(
    blocks_ref, held_bands, out_ref, src, near0, near1, near2, near3, held, far, mine, full,
    send1, recv1, own1, relay, relay_send, relay_recv, send2, recv2, send3, recv3, send4, recv4,
):
    band = lax.axis_index("band")
    z, x = band // SIDE, band % SIDE
    near = (near0, near1, near2, near3)

    def along_x(k):
        return {"band": z * SIDE + (x + k) % SIDE}

    def along_z(k):
        return {"band": (z + k) % SIDE * SIDE + x}

    def lanes(q, s):
        return pl.ds(pl.multiple_of(q % 2 * PART + s * PIECE, 128), PIECE)

    count = held_bands.shape[1]
    for b in range(2):
        src[b] = held_bands[:, lax.rem(blocks_ref[b], count)]
    greet([along_x(k) for k in (1, 2, 3)] + [along_z(k) for k in (1, 2, 3)])
    order = (2, 1, 3, 0)
    first = {}
    for j in order:
        s = (z + j) % SIDE
        way = 1 if j in (1, 2) else 3
        q = (x + 2) % SIDE
        copy = remote(
            src.at[q // 2, :, :, lanes(q, s)], relay.at[j],
            relay_send.at[j], relay_recv.at[j], along_x(way),
        )
        copy.start()
        first[j, "relay"] = copy
        for k in (1, 3):
            q = (x + k) % SIDE
            copy = remote(
                src.at[q // 2, :, :, lanes(q, s)], near[j].at[x],
                send1.at[j, k - 1], recv1.at[j, k - 1], along_x(k),
            )
            copy.start()
            first[j, k] = copy
        copy = pltpu.make_async_copy(src.at[x // 2, :, :, lanes(x, s)], near[j].at[x], own1.at[j])
        copy.start()
        first[j, 0] = copy
    owner = lax.div(blocks_ref[x // 2], count)
    owner_z, owner_x = owner // SIDE, owner % SIDE
    second = []

    def forward(j):
        way = 1 if j in (1, 2) else 3
        first[j, "relay"].wait()
        copy = remote(
            relay.at[j], near[j].at[(x + SIDE - way) % SIDE],
            send1.at[j, 1], recv1.at[j, 1], along_x(way),
        )
        copy.start()
        first[j, 2] = copy

    forward(order[0])
    for i, j in enumerate(order):
        if i + 1 < SIDE:
            forward(order[i + 1])
        for k in range(SIDE):
            first[j, k].wait()
        if j == 0:
            far[z] = near[j][owner_x]
        else:
            held[j] = near[j][owner_x]
            copy = remote(
                held.at[j], far.at[z], send2.at[j - 1], recv2.at[j - 1], along_z(j)
            )
            copy.start()
            second.append(copy)
    for copy in second:
        copy.wait()
    picked = far[owner_z]
    mine[...] = picked
    full[x // 2, :, :, lanes(x, z)] = picked
    third = {}
    for k in (2, 1, 3):
        copy = remote(
            mine, full.at[x // 2, :, :, lanes(x, z)], send3.at[k - 1], recv3.at[k - 1], along_z(k)
        )
        copy.start()
        third[k] = copy
    fourth = []
    for j in (0, 1, 3, 2):
        if j:
            third[j].wait()
        s = (z + SIDE - j) % SIDE
        part = full.at[x // 2, :, :, lanes(x, s)]
        for k in (1, 3):
            copy = remote(
                mine if j == 0 else part, part, send4.at[j, k - 1], recv4.at[j, k - 1], along_x(k)
            )
            copy.start()
            fourth.append((j, k, copy))
    passed = []
    for j in (0, 1, 3, 2):
        way = 1 if j in (0, 1) else 3
        came = (x + SIDE - way) % SIDE
        part = full.at[came // 2, :, :, lanes(came, (z + SIDE - j) % SIDE)]
        remote(
            part, part, send4.at[j, way - 1], recv4.at[j, way - 1], along_x(way)
        ).wait_recv()
        copy = remote(part, part, send4.at[j, 1], recv4.at[j, 1], along_x(way))
        copy.start()
        passed.append(copy)
    for j, k, copy in fourth:
        copy.wait_send()
        if k != (1 if j in (0, 1) else 3):
            copy.wait_recv()
    for copy in passed:
        copy.wait()
    out_ref[...] = full[...]


def spread(blocks, held_bands):
    planes = held_bands.shape[0]
    whole = (2, planes, BLK, LANES)
    piece = (planes, BLK, PIECE)
    dma = pltpu.SemaphoreType.DMA
    vmem = pl.BlockSpec(memory_space=pltpu.VMEM)
    return pl.pallas_call(
        spread_kernel,
        out_shape=jax.ShapeDtypeStruct(whole, jnp.bfloat16),
        in_specs=[pl.BlockSpec(memory_space=pltpu.SMEM), vmem],
        out_specs=vmem,
        scratch_shapes=[
            pltpu.VMEM(whole, jnp.bfloat16),
            *[pltpu.VMEM((SIDE, *piece), jnp.bfloat16) for _ in range(SIDE)],
            pltpu.VMEM((SIDE, *piece), jnp.bfloat16),
            pltpu.VMEM((SIDE, *piece), jnp.bfloat16),
            pltpu.VMEM(piece, jnp.bfloat16),
            pltpu.VMEM(whole, jnp.bfloat16),
            dma((SIDE, 3)), dma((SIDE, 3)), dma((SIDE,)),
            pltpu.VMEM((SIDE, *piece), jnp.bfloat16), dma((SIDE,)), dma((SIDE,)),
            dma((3,)), dma((3,)), dma((3,)), dma((3,)),
            dma((SIDE, 3)), dma((SIDE, 3)),
        ],
        compiler_params=pltpu.CompilerParams(collective_id=0, has_side_effects=True),
        name="spread_blocks",
    )(blocks, held_bands)


def density_kernel(
    devices, chosen, cond, z_mat, mix, points, out_ref, twin_points, sections, made,
    send, recv, own, point_send, point_recv,
):
    me = lax.axis_index("grid")
    half = devices // 2
    ring = half // 2
    z, y, c = me // half, me % half // 2, me % 2
    planes = cond.shape[0]
    barrier = pltpu.get_barrier_semaphore()
    for k in range(1, devices):
        pl.semaphore_signal(
            barrier, inc=1, device_id={"grid": (me + k) % devices}, device_id_type=MESH
        )

    def compute(x):
        def z_step(j, carry):
            both = []
            for part in range(2):
                at = pl.ds(pl.multiple_of((2 * j + part) * CHUNK, 128), CHUNK)
                cc = cond[x, :, at].astype(jnp.float32)
                v = jnp.concatenate(
                    [chosen[0, x, :, at].astype(jnp.float32), chosen[1, x, :, at].astype(jnp.float32)]
                )
                dens = (v[:, None, :] * cc[None, :, :]).reshape(2 * PAIRS, CHUNK)
                summed = lax.dot_general(
                    z_mat[...], dens.astype(jnp.bfloat16), (((1,), (1,)), ((), ())),
                    preferred_element_type=jnp.float32,
                )
                both.append(summed.reshape(NEG, 2 * ROWS_Y, 2 * PAIRS))
            joined = jnp.concatenate(both, axis=1).astype(jnp.bfloat16)
            sections[:, pl.ds(pl.multiple_of(j * 4 * ROWS_Y, 16), 4 * ROWS_Y), :] = joined
            return carry

        lax.fori_loop(0, LANES // CHUNK // 2, z_step, 0)
        made[x, :, NEG] = jnp.zeros((KF, 2, 2 * PAIRS), jnp.bfloat16)

        for q in range(NEG):
            value = jnp.dot(
                mix[...], sections[q], preferred_element_type=jnp.float32
            ).astype(jnp.bfloat16)
            made[x, :, q] = value[: 2 * KF].reshape(KF, 2, 2 * PAIRS)
            made[x, NEG - 1 - q, NEG] = value[2 * KF :]

    def moves(x):
        for dy in sorted(range(ring), key=lambda d: -min(d, ring - d)):
            for dz in (1, 0):
                for dc in (0, 1):
                    k = dz * half + dy * 2 + dc
                    if k:
                        to = (z + dz) % 2 * half + (y + dy) % ring * 2 + (c + dc) % 2
                        source = (z + dz) % 2 * half + (y + ring - dy) % ring * 2 + (c + dc) % 2
                        yield k, to, source

    def post(x):
        for k, to, _ in moves(x):
            remote(
                made.at[x, to], out_ref.at[me, x], send.at[x, k], recv.at[x, k], {"grid": to}
            ).start()
        pltpu.make_async_copy(made.at[x, me], out_ref.at[me, x], own.at[x]).start()

    compute(0)
    pl.semaphore_wait(barrier, devices - 1)
    post(0)
    paired = (me != 0) & (me != half)
    swap = remote(
        points, twin_points, point_send.at[0], point_recv.at[0], {"grid": (devices - me) % devices}
    )
    keep = pltpu.make_async_copy(points, twin_points, point_send.at[0])

    @pl.when(paired)
    def _():
        swap.start()

    @pl.when(jnp.logical_not(paired))
    def _():
        keep.start()
        keep.wait()

    def plane(x, carry):
        compute(x)
        post(x)
        return carry

    lax.fori_loop(1, planes, plane, 0)

    def finish(x, carry):
        for k, to, source in moves(x):
            remote(
                made.at[x, to], out_ref.at[source, x], send.at[x, k], recv.at[x, k], {"grid": to}
            ).wait()
        pltpu.make_async_copy(made.at[x, me], out_ref.at[me, x], own.at[x]).wait()
        return carry

    lax.fori_loop(0, planes, finish, 0)

    @pl.when(paired)
    def _():
        swap.wait()


def densities(chosen, cond, z_mat, mix, points, devices):
    planes = cond.shape[0]
    dma = pltpu.SemaphoreType.DMA
    vmem = pl.BlockSpec(memory_space=pltpu.VMEM)
    anywhere = pl.BlockSpec(memory_space=pl.ANY)
    return pl.pallas_call(
        functools.partial(density_kernel, devices),
        out_shape=[
            jax.ShapeDtypeStruct((devices, planes, NEG + 1, 2, 2 * PAIRS), jnp.bfloat16),
            jax.ShapeDtypeStruct(points.shape, points.dtype),
        ],
        in_specs=[vmem] * 4 + [anywhere],
        out_specs=[anywhere] * 2,
        scratch_shapes=[
            pltpu.VMEM((NEG, 2 * GRID_N, 2 * PAIRS), jnp.bfloat16),
            pltpu.VMEM((planes, devices, NEG + 1, 2, 2 * PAIRS), jnp.bfloat16),
            dma((planes, devices)), dma((planes, devices)), dma((planes,)), dma((1,)), dma((1,)),
        ],
        compiler_params=pltpu.CompilerParams(collective_id=2, has_side_effects=True),
        name="density_and_exchange",
    )(chosen, cond, z_mat, mix, points)


def one_hot(index, count):
    rows = lax.broadcasted_iota(jnp.int32, (count, index.shape[1]), 0)
    return jnp.where(rows == index, 1.0, 0.0).astype(jnp.bfloat16)


def pick(index, table):
    return lax.dot_general(
        one_hot(index, table.shape[0]), table, (((0,), (0,)), ((), ())),
        preferred_element_type=jnp.float32,
    )


def sphere_rows(moved, mix, points, twin_points, own_rows, twin_rows, table_ref, table):
    for q in range(NEG + 1):
        rows = moved[:, :, q].reshape(2 * GRID_N, 2 * PAIRS)
        part = jnp.dot(mix[...], rows, preferred_element_type=jnp.float32)
        both = jnp.concatenate([part[:ROWS_X], part[ROWS_X:]], axis=1).astype(jnp.bfloat16)
        if q < NEG:
            table[q * ROWS_X : (q + 1) * ROWS_X] = both
        else:
            table_ref[...] = both[:KF]
    qx, qz = lax.div(points, KF), lax.rem(points, KF)
    twin_qx, twin_qz = lax.div(twin_points, KF), lax.rem(twin_points, KF)
    own_at = jnp.where(qz < NEG, qz * ROWS_X + qx, -1)
    twin_at = jnp.where(twin_qz < NEG, -1, (KF - twin_qz) * ROWS_X + KF - twin_qx)
    own_rows[...] = pick(own_at, table[...]).astype(jnp.bfloat16)
    twin = pick(twin_at, table[...])
    lanes = lax.broadcasted_iota(jnp.int32, twin.shape, 1)
    twin_rows[...] = jnp.where(lanes < 2 * PAIRS, twin, -twin).astype(jnp.bfloat16)
    return jnp.where(qz < NEG, -1, (qz - NEG) * KF + qx)


def tail_kernel(
    devices, moved, mix, points, twin_points, screened, out_ref,
    own_rows, twin_rows, table, found, weights, total, got, tables, side_a, side_b, rows, parts, arrived,
    swap_send, swap_recv, lone_send, lone_recv, send, recv, own, sum_send, sum_recv, fetched,
):
    fetch = pltpu.make_async_copy(screened, weights, fetched.at[0])
    fetch.start()
    me = lax.axis_index("grid")
    half = devices // 2
    ring = half // 2
    z, y, c = me // half, me % half // 2, me % 2

    def at(zz, yy, cc):
        return zz * half + yy % ring * 2 + cc

    barrier = pltpu.get_barrier_semaphore()
    for k in range(1, devices):
        pl.semaphore_signal(
            barrier, inc=1, device_id={"grid": (me + k) % devices}, device_id_type=MESH
        )
    lone_at = sphere_rows(
        moved, mix, points[...], twin_points[...], own_rows, twin_rows, table, found
    )
    pl.semaphore_wait(barrier, devices - 1)
    paired = (me != 0) & (me != half)
    swap = remote(
        twin_rows, got, swap_send.at[0], swap_recv.at[0], {"grid": (devices - me) % devices}
    )
    helper = (me > 0) & (me < half)

    @pl.when(helper)
    def _():
        remote(
            table, tables.at[me - 1], lone_send.at[0], lone_recv.at[me - 1], {"grid": 0}
        ).start()

    @pl.when(paired)
    def _():
        swap.start()
        swap.wait()

    @pl.when(me == half)
    def _():
        got[...] = twin_rows[...]

    @pl.when(me == 0)
    def _():
        for i in range(half - 1):
            remote(
                table, tables.at[i], lone_send.at[0], lone_recv.at[i], {"grid": i + 1}
            ).wait_recv()
        count = (half - 1) * KF
        picked = pick(lone_at, tables[...].reshape(count, 4 * PAIRS))
        got[...] = picked.astype(jnp.bfloat16)

    @pl.when(helper)
    def _():
        remote(
            table, tables.at[me - 1], lone_send.at[0], lone_recv.at[me - 1], {"grid": 0}
        ).wait_send()

    sphere = own_rows[...].astype(jnp.float32) + got[...].astype(jnp.float32)
    real, imag = sphere[:, : 2 * PAIRS], sphere[:, 2 * PAIRS :]
    side_b[...] = jnp.concatenate([real[:, PAIRS:], imag[:, PAIRS:]], axis=1).astype(jnp.bfloat16)
    side_a[...] = jnp.concatenate([real[:, :PAIRS], imag[:, :PAIRS]], axis=1).astype(jnp.bfloat16)
    local = pltpu.make_async_copy(side_b, rows.at[me], own.at[0])
    local.start()
    started = []

    def push(slot, peer, from_input=False):
        copy = remote(
            side_b if from_input else rows.at[slot], rows.at[slot],
            send.at[len(started)], recv.at[slot], {"grid": peer},
        )
        copy.start()
        started.append(copy)

    def landed(slot):
        pltpu.make_async_remote_copy(
            src_ref=rows.at[slot], dst_ref=rows.at[slot], send_sem=own.at[0],
            recv_sem=recv.at[slot], device_id={"grid": at(z, y, 1 - c)}, device_id_type=MESH,
        ).wait_recv()

    up, down, twin = at(z, y + 1, c), at(z, y + ring - 1, c), at(z, y, 1 - c)
    push(me, at(1 - z, y, c), True)
    push(me, up, True)
    push(me, down, True)
    push(me, twin, True)
    other = at(1 - z, y, c)
    landed(other)
    push(other, up)
    push(other, down)
    push(other, twin)
    count = side_a.shape[0]
    total[...] = jnp.zeros_like(total)
    local.wait()
    fetch.wait()

    def screen(zz, back):
        landed(at(zz, y + back, 1 - c))
        first = at(zz, y + back, 0)
        columns = pl.ds(pl.multiple_of(first * count, 128), 2 * count)
        pair = rows[pl.ds(first, 2)].reshape(2 * count, 2 * PAIRS)
        total[...] += jnp.dot(weights[:, columns], pair, preferred_element_type=jnp.float32)

    ready = [(z, 0), (1 - z, 0)]
    for t in range(1, ring // 2 + 1):
        fresh = []
        for zz, ups in ((z, ring // 2), (1 - z, ring // 2 - 1)):
            for steps, back, peer in ((ups, ring - t, up), (ring - 1 - ups, t, down)):
                if t <= steps:
                    slot = at(zz, y + back, c)
                    landed(slot)
                    if t < steps:
                        push(slot, peer)
                    push(slot, twin)
                    fresh.append((zz, back))
        for pair in ready:
            screen(*pair)
        ready = fresh
    for pair in ready:
        screen(*pair)
    product = lax.dot_general(
        side_a[...], total[...].astype(jnp.bfloat16), (((0,), (0,)), ((), ())), preferred_element_type=jnp.float32
    )
    value = product[:PAIRS, :PAIRS] + product[PAIRS:, PAIRS:]
    width = PAIRS // devices
    for g in range(devices):
        parts[g] = value[g * width : (g + 1) * width]
    for copy in started:
        copy.wait_send()
    moves = []
    for k in range(1, devices):
        peer = (me + k) % devices
        copy = remote(
            parts.at[peer], arrived.at[k], sum_send.at[k], sum_recv.at[k], {"grid": peer}
        )
        copy.start()
        moves.append(copy)
    result = parts[me]
    for copy in moves:
        copy.wait()
    for k in range(1, devices):
        result = result + arrived[k]
    out_ref[...] = result


def tail(moved, mix, points, twin_points, screened, devices):
    vmem = pl.BlockSpec(memory_space=pltpu.VMEM)
    dma = pltpu.SemaphoreType.DMA
    width = PAIRS // devices
    side = (points.shape[1], 2 * PAIRS)
    both = (points.shape[1], 4 * PAIRS)
    table = (KF, 4 * PAIRS)
    return pl.pallas_call(
        functools.partial(tail_kernel, devices),
        out_shape=jax.ShapeDtypeStruct((width, PAIRS), jnp.float32),
        in_specs=[vmem] * 4 + [pl.BlockSpec(memory_space=pl.ANY)],
        out_specs=vmem,
        scratch_shapes=[
            pltpu.VMEM(both, jnp.bfloat16),
            pltpu.VMEM(both, jnp.bfloat16),
            pltpu.VMEM(table, jnp.bfloat16),
            pltpu.VMEM((NEG * ROWS_X, 4 * PAIRS), jnp.bfloat16),
            pltpu.VMEM(screened.shape, jnp.bfloat16),
            pltpu.VMEM(side, jnp.float32),
            pltpu.VMEM(both, jnp.bfloat16),
            pltpu.VMEM((devices // 2 - 1, *table), jnp.bfloat16),
            pltpu.VMEM(side, jnp.bfloat16),
            pltpu.VMEM(side, jnp.bfloat16),
            pltpu.VMEM((devices, *side), jnp.bfloat16),
            pltpu.VMEM((devices, width, PAIRS), jnp.float32),
            pltpu.VMEM((devices, width, PAIRS), jnp.float32),
            dma((1,)), dma((1,)), dma((1,)), dma((devices // 2 - 1,)),
            dma((devices,)), dma((devices,)), dma((1,)), dma((devices,)), dma((devices,)),
            dma((1,)),
        ],
        compiler_params=pltpu.CompilerParams(collective_id=1, has_side_effects=True),
        name="screen_and_sum",
    )(moved, mix, points, twin_points, screened)


def per_device(devices, valence, conduction, screened, blocks, gsphere):
    held_blocks = valence.shape[0] // BLK
    planes = conduction.shape[1]
    by_plane = jnp.transpose(valence, (1, 0, 2)).reshape(planes, held_blocks, BLK, LANES)
    chosen = spread(blocks, by_plane)
    points = gsphere[None]
    moved, twin_points = densities(
        chosen, jnp.transpose(conduction, (1, 0, 2)), jnp.asarray(z_matrix()),
        jnp.asarray(y_matrix()), points, devices,
    )
    return tail(moved, jnp.asarray(x_matrix()), points, twin_points, screened, devices)[None]


def solution(mesh):
    in_specs = (P("band", "grid", None), P("band", "grid", None), P("grid", None), P(), P("grid"))
    return jax.shard_map(
        functools.partial(per_device, mesh.shape["grid"]), mesh=mesh, in_specs=in_specs,
        out_specs=P("band", "grid", None), check_vma=False,
    )
```

```python
import functools
import math

import jax
import jax.numpy as jnp
import ml_dtypes
import numpy as np
from jax import lax
from jax.experimental import pallas as pl
from jax.experimental.pallas import tpu as pltpu
from jax.sharding import PartitionSpec as P

GRID_N = 96
KF = 32
BLK = 8
PAIRS = 64
SIDE = 4
LANES = GRID_N * GRID_N
PART = LANES // 2
PIECE = PART // SIDE
ROWS_Y = 4
CHUNK = ROWS_Y * GRID_N
NEG = KF // 2 + 1
FULL_X = KF + 1
ROWS_X = 48
MESH = pl.DeviceIdType.MESH


def fourier_parts(length, kept):
    positions = np.arange(length)
    freqs = np.arange(kept) - KF // 2
    phases = (positions[:, None] * freqs[None, :] % length) * (2.0 * math.pi / length)
    factor = 1.0 / math.sqrt(length)
    return np.cos(phases) * factor, np.sin(phases) * factor


def first_table():
    cosine, sine = fourier_parts(GRID_N, KF)
    return np.stack([cosine, -sine], axis=2)


def mixing_table(kept):
    cosine, sine = fourier_parts(GRID_N, kept)
    real_rows = np.stack([cosine, sine], axis=-1)
    imag_rows = np.stack([-sine, cosine], axis=-1)
    return np.stack([real_rows, imag_rows], axis=2)


def z_matrix():
    table = first_table()[:, :NEG]
    out = np.zeros((NEG, ROWS_Y, 2, ROWS_Y, GRID_N))
    for y in range(ROWS_Y):
        out[:, y, :, y, :] = np.transpose(table, (1, 2, 0))
    return out.reshape(NEG * ROWS_Y * 2, CHUNK).astype(ml_dtypes.bfloat16)


def y_matrix():
    table = np.transpose(mixing_table(KF), (1, 2, 0, 3))
    lowest = table[:1] * np.array([1.0, -1.0])
    return np.concatenate([table, lowest]).reshape(2 * KF + 2, 2 * GRID_N).astype(ml_dtypes.bfloat16)


def x_matrix():
    table = np.transpose(mixing_table(FULL_X), (2, 1, 0, 3)).reshape(2, FULL_X, 2 * GRID_N)
    out = np.zeros((2, ROWS_X, 2 * GRID_N))
    out[:, :FULL_X] = table
    return out.reshape(2 * ROWS_X, 2 * GRID_N).astype(ml_dtypes.bfloat16)


def remote(src, dst, send, recv, peer):
    return pltpu.make_async_remote_copy(
        src_ref=src, dst_ref=dst, send_sem=send, recv_sem=recv, device_id=peer, device_id_type=MESH
    )


def greet(peers):
    barrier = pltpu.get_barrier_semaphore()
    for peer in peers:
        pl.semaphore_signal(barrier, inc=1, device_id=peer, device_id_type=MESH)
    pl.semaphore_wait(barrier, len(peers))


def spread_kernel(
    blocks_ref, held_bands, out_ref, src, near0, near1, near2, near3, held, far, mine, full,
    send1, recv1, own1, send2, recv2, send3, recv3, send4, recv4,
):
    band = lax.axis_index("band")
    z, x = band // SIDE, band % SIDE
    near = (near0, near1, near2, near3)

    def along_x(k):
        return {"band": z * SIDE + (x + k) % SIDE}

    def along_z(k):
        return {"band": (z + k) % SIDE * SIDE + x}

    def lanes(q, s):
        return pl.ds(pl.multiple_of(q % 2 * PART + s * PIECE, 128), PIECE)

    count = held_bands.shape[1]
    for b in range(2):
        src[b] = held_bands[:, lax.rem(blocks_ref[b], count)]
    greet([along_x(k) for k in (1, 2, 3)] + [along_z(k) for k in (1, 2, 3)])
    order = (2, 1, 3, 0)
    first = {}
    for j in order:
        s = (z + j) % SIDE
        for k in (2, 1, 3):
            q = (x + k) % SIDE
            copy = remote(
                src.at[q // 2, :, :, lanes(q, s)], near[j].at[x],
                send1.at[j, k - 1], recv1.at[j, k - 1], along_x(k),
            )
            copy.start()
            first[j, k] = copy
        copy = pltpu.make_async_copy(src.at[x // 2, :, :, lanes(x, s)], near[j].at[x], own1.at[j])
        copy.start()
        first[j, 0] = copy
    owner = lax.div(blocks_ref[x // 2], count)
    owner_z, owner_x = owner // SIDE, owner % SIDE
    second = []
    for j in order:
        for k in range(SIDE):
            first[j, k].wait()
        if j == 0:
            far[z] = near[j][owner_x]
        else:
            held[j] = near[j][owner_x]
            copy = remote(
                held.at[j], far.at[z], send2.at[j - 1], recv2.at[j - 1], along_z(j)
            )
            copy.start()
            second.append(copy)
    for copy in second:
        copy.wait_recv()
    picked = far[owner_z]
    mine[...] = picked
    full[x // 2, :, :, lanes(x, z)] = picked
    third = {}
    for k in (2, 1, 3):
        copy = remote(
            mine, full.at[x // 2, :, :, lanes(x, z)], send3.at[k - 1], recv3.at[k - 1], along_z(k)
        )
        copy.start()
        third[k] = copy
    fourth = []
    for j in (0, 1, 3, 2):
        if j:
            third[j].wait_recv()
        s = (z + SIDE - j) % SIDE
        part = full.at[x // 2, :, :, lanes(x, s)]
        for k in (2, 1, 3):
            copy = remote(
                mine if j == 0 else part, part, send4.at[j, k - 1], recv4.at[j, k - 1], along_x(k)
            )
            copy.start()
            fourth.append(copy)
    for copy in fourth:
        copy.wait()
    for copy in second + list(third.values()):
        copy.wait_send()
    out_ref[...] = full[...]


def spread(blocks, held_bands):
    planes = held_bands.shape[0]
    whole = (2, planes, BLK, LANES)
    piece = (planes, BLK, PIECE)
    dma = pltpu.SemaphoreType.DMA
    vmem = pl.BlockSpec(memory_space=pltpu.VMEM)
    return pl.pallas_call(
        spread_kernel,
        out_shape=jax.ShapeDtypeStruct(whole, jnp.bfloat16),
        in_specs=[pl.BlockSpec(memory_space=pltpu.SMEM), vmem],
        out_specs=vmem,
        scratch_shapes=[
            pltpu.VMEM(whole, jnp.bfloat16),
            *[pltpu.VMEM((SIDE, *piece), jnp.bfloat16) for _ in range(SIDE)],
            pltpu.VMEM((SIDE, *piece), jnp.bfloat16),
            pltpu.VMEM((SIDE, *piece), jnp.bfloat16),
            pltpu.VMEM(piece, jnp.bfloat16),
            pltpu.VMEM(whole, jnp.bfloat16),
            dma((SIDE, 3)), dma((SIDE, 3)), dma((SIDE,)),
            dma((3,)), dma((3,)), dma((3,)), dma((3,)),
            dma((SIDE, 3)), dma((SIDE, 3)),
        ],
        compiler_params=pltpu.CompilerParams(collective_id=0, has_side_effects=True),
        name="spread_blocks",
    )(blocks, held_bands)


def density_kernel(
    devices, chosen, cond, z_mat, mix, points, out_ref, twin_points, sections, made,
    send, recv, own, point_send, point_recv,
):
    me = lax.axis_index("grid")
    half = devices // 2
    ring = half // 2
    z, y, c = me // half, me % half // 2, me % 2
    planes = cond.shape[0]
    barrier = pltpu.get_barrier_semaphore()
    for k in range(1, devices):
        pl.semaphore_signal(
            barrier, inc=1, device_id={"grid": (me + k) % devices}, device_id_type=MESH
        )

    def compute(x):
        def z_step(j, carry):
            both = []
            for part in range(2):
                at = pl.ds(pl.multiple_of((2 * j + part) * CHUNK, 128), CHUNK)
                cc = cond[x, :, at].astype(jnp.float32)
                v = jnp.concatenate(
                    [chosen[0, x, :, at].astype(jnp.float32), chosen[1, x, :, at].astype(jnp.float32)]
                )
                dens = (v[:, None, :] * cc[None, :, :]).reshape(2 * PAIRS, CHUNK)
                summed = lax.dot_general(
                    z_mat[...], dens.astype(jnp.bfloat16), (((1,), (1,)), ((), ())),
                    preferred_element_type=jnp.float32,
                )
                both.append(summed.reshape(NEG, 2 * ROWS_Y, 2 * PAIRS))
            joined = jnp.concatenate(both, axis=1).astype(jnp.bfloat16)
            sections[:, pl.ds(pl.multiple_of(j * 4 * ROWS_Y, 16), 4 * ROWS_Y), :] = joined
            return carry

        lax.fori_loop(0, LANES // CHUNK // 2, z_step, 0)
        made[x, :, NEG] = jnp.zeros((KF, 2, 2 * PAIRS), jnp.bfloat16)

        for q in range(NEG):
            value = jnp.dot(
                mix[...], sections[q], preferred_element_type=jnp.float32
            ).astype(jnp.bfloat16)
            made[x, :, q] = value[: 2 * KF].reshape(KF, 2, 2 * PAIRS)
            made[x, NEG - 1 - q, NEG] = value[2 * KF :]

    def moves(x):
        for dy in sorted(range(ring), key=lambda d: -min(d, ring - d)):
            for dz in (1, 0):
                for dc in (0, 1):
                    k = dz * half + dy * 2 + dc
                    if k:
                        to = (z + dz) % 2 * half + (y + dy) % ring * 2 + (c + dc) % 2
                        source = (z + dz) % 2 * half + (y + ring - dy) % ring * 2 + (c + dc) % 2
                        yield k, to, source

    def post(x):
        for k, to, _ in moves(x):
            remote(
                made.at[x, to], out_ref.at[me, x], send.at[x, k], recv.at[x, k], {"grid": to}
            ).start()
        pltpu.make_async_copy(made.at[x, me], out_ref.at[me, x], own.at[x]).start()

    compute(0)
    pl.semaphore_wait(barrier, devices - 1)
    post(0)
    paired = (me != 0) & (me != half)
    swap = remote(
        points, twin_points, point_send.at[0], point_recv.at[0], {"grid": (devices - me) % devices}
    )
    keep = pltpu.make_async_copy(points, twin_points, point_send.at[0])

    @pl.when(paired)
    def _():
        swap.start()

    @pl.when(jnp.logical_not(paired))
    def _():
        keep.start()
        keep.wait()

    def plane(x, carry):
        compute(x)
        post(x)
        return carry

    lax.fori_loop(1, planes, plane, 0)

    def finish(x, carry):
        for k, to, source in moves(x):
            remote(
                made.at[x, to], out_ref.at[source, x], send.at[x, k], recv.at[x, k], {"grid": to}
            ).wait()
        pltpu.make_async_copy(made.at[x, me], out_ref.at[me, x], own.at[x]).wait()
        return carry

    lax.fori_loop(0, planes, finish, 0)

    @pl.when(paired)
    def _():
        swap.wait()


def densities(chosen, cond, z_mat, mix, points, devices):
    planes = cond.shape[0]
    dma = pltpu.SemaphoreType.DMA
    vmem = pl.BlockSpec(memory_space=pltpu.VMEM)
    anywhere = pl.BlockSpec(memory_space=pl.ANY)
    return pl.pallas_call(
        functools.partial(density_kernel, devices),
        out_shape=[
            jax.ShapeDtypeStruct((devices, planes, NEG + 1, 2, 2 * PAIRS), jnp.bfloat16),
            jax.ShapeDtypeStruct(points.shape, points.dtype),
        ],
        in_specs=[vmem] * 4 + [anywhere],
        out_specs=[anywhere] * 2,
        scratch_shapes=[
            pltpu.VMEM((NEG, 2 * GRID_N, 2 * PAIRS), jnp.bfloat16),
            pltpu.VMEM((planes, devices, NEG + 1, 2, 2 * PAIRS), jnp.bfloat16),
            dma((planes, devices)), dma((planes, devices)), dma((planes,)), dma((1,)), dma((1,)),
        ],
        compiler_params=pltpu.CompilerParams(collective_id=2, has_side_effects=True),
        name="density_and_exchange",
    )(chosen, cond, z_mat, mix, points)


def one_hot(index, count):
    rows = lax.broadcasted_iota(jnp.int32, (count, index.shape[1]), 0)
    return jnp.where(rows == index, 1.0, 0.0).astype(jnp.bfloat16)


def pick(index, table):
    return lax.dot_general(
        one_hot(index, table.shape[0]), table, (((0,), (0,)), ((), ())),
        preferred_element_type=jnp.float32,
    )


def sphere_rows(moved, mix, points, twin_points, own_rows, twin_rows, table_ref, table):
    for q in range(NEG + 1):
        rows = moved[:, :, q].reshape(2 * GRID_N, 2 * PAIRS)
        part = jnp.dot(mix[...], rows, preferred_element_type=jnp.float32)
        both = jnp.concatenate([part[:ROWS_X], part[ROWS_X:]], axis=1).astype(jnp.bfloat16)
        if q < NEG:
            table[q * ROWS_X : (q + 1) * ROWS_X] = both
        else:
            table_ref[...] = both[:KF]
    qx, qz = lax.div(points, KF), lax.rem(points, KF)
    twin_qx, twin_qz = lax.div(twin_points, KF), lax.rem(twin_points, KF)
    own_at = jnp.where(qz < NEG, qz * ROWS_X + qx, -1)
    twin_at = jnp.where(twin_qz < NEG, -1, (KF - twin_qz) * ROWS_X + KF - twin_qx)
    own_rows[...] = pick(own_at, table[...]).astype(jnp.bfloat16)
    twin = pick(twin_at, table[...])
    lanes = lax.broadcasted_iota(jnp.int32, twin.shape, 1)
    twin_rows[...] = jnp.where(lanes < 2 * PAIRS, twin, -twin).astype(jnp.bfloat16)
    return jnp.where(qz < NEG, -1, (qz - NEG) * KF + qx)


def tail_kernel(
    devices, moved, mix, points, twin_points, screened, out_ref,
    own_rows, twin_rows, table, found, weights, total, got, tables, side_a, side_b, rows, parts, arrived,
    swap_send, swap_recv, lone_send, lone_recv, send, recv, own, sum_send, sum_recv, fetched,
):
    fetch = pltpu.make_async_copy(screened, weights, fetched.at[0])
    fetch.start()
    me = lax.axis_index("grid")
    half = devices // 2
    ring = half // 2
    z, y, c = me // half, me % half // 2, me % 2

    def at(zz, yy, cc):
        return zz * half + yy % ring * 2 + cc

    barrier = pltpu.get_barrier_semaphore()
    for k in range(1, devices):
        pl.semaphore_signal(
            barrier, inc=1, device_id={"grid": (me + k) % devices}, device_id_type=MESH
        )
    lone_at = sphere_rows(
        moved, mix, points[...], twin_points[...], own_rows, twin_rows, table, found
    )
    pl.semaphore_wait(barrier, devices - 1)
    paired = (me != 0) & (me != half)
    swap = remote(
        twin_rows, got, swap_send.at[0], swap_recv.at[0], {"grid": (devices - me) % devices}
    )
    helper = (me > 0) & (me < half)

    @pl.when(helper)
    def _():
        remote(
            table, tables.at[me - 1], lone_send.at[0], lone_recv.at[me - 1], {"grid": 0}
        ).start()

    @pl.when(paired)
    def _():
        swap.start()
        swap.wait()

    @pl.when(me == half)
    def _():
        got[...] = twin_rows[...]

    @pl.when(me == 0)
    def _():
        for i in range(half - 1):
            remote(
                table, tables.at[i], lone_send.at[0], lone_recv.at[i], {"grid": i + 1}
            ).wait_recv()
        count = (half - 1) * KF
        picked = pick(lone_at, tables[...].reshape(count, 4 * PAIRS))
        got[...] = picked.astype(jnp.bfloat16)

    @pl.when(helper)
    def _():
        remote(
            table, tables.at[me - 1], lone_send.at[0], lone_recv.at[me - 1], {"grid": 0}
        ).wait_send()

    sphere = own_rows[...].astype(jnp.float32) + got[...].astype(jnp.float32)
    real, imag = sphere[:, : 2 * PAIRS], sphere[:, 2 * PAIRS :]
    side_b[...] = jnp.concatenate([real[:, PAIRS:], imag[:, PAIRS:]], axis=1).astype(jnp.bfloat16)
    side_a[...] = jnp.concatenate([real[:, :PAIRS], imag[:, :PAIRS]], axis=1).astype(jnp.bfloat16)
    local = pltpu.make_async_copy(side_b, rows.at[me], own.at[0])
    local.start()
    started = []

    def push(slot, peer, from_input=False):
        copy = remote(
            side_b if from_input else rows.at[slot], rows.at[slot],
            send.at[len(started)], recv.at[slot], {"grid": peer},
        )
        copy.start()
        started.append(copy)

    def landed(slot):
        pltpu.make_async_remote_copy(
            src_ref=rows.at[slot], dst_ref=rows.at[slot], send_sem=own.at[0],
            recv_sem=recv.at[slot], device_id={"grid": at(z, y, 1 - c)}, device_id_type=MESH,
        ).wait_recv()

    up, down, twin = at(z, y + 1, c), at(z, y + ring - 1, c), at(z, y, 1 - c)
    push(me, at(1 - z, y, c), True)
    push(me, up, True)
    push(me, down, True)
    push(me, twin, True)
    other = at(1 - z, y, c)
    landed(other)
    push(other, up)
    push(other, down)
    push(other, twin)
    count = side_a.shape[0]
    total[...] = jnp.zeros_like(total)
    local.wait()
    fetch.wait()

    def screen(zz, back):
        landed(at(zz, y + back, 1 - c))
        first = at(zz, y + back, 0)
        columns = pl.ds(pl.multiple_of(first * count, 128), 2 * count)
        pair = rows[pl.ds(first, 2)].reshape(2 * count, 2 * PAIRS)
        total[...] += jnp.dot(weights[:, columns], pair, preferred_element_type=jnp.float32)

    ready = [(z, 0), (1 - z, 0)]
    for t in range(1, ring // 2 + 1):
        fresh = []
        for zz, ups in ((z, ring // 2), (1 - z, ring // 2 - 1)):
            for steps, back, peer in ((ups, ring - t, up), (ring - 1 - ups, t, down)):
                if t <= steps:
                    slot = at(zz, y + back, c)
                    landed(slot)
                    if t < steps:
                        push(slot, peer)
                    push(slot, twin)
                    fresh.append((zz, back))
        for pair in ready:
            screen(*pair)
        ready = fresh
    for pair in ready:
        screen(*pair)
    product = lax.dot_general(
        side_a[...], total[...].astype(jnp.bfloat16), (((0,), (0,)), ((), ())), preferred_element_type=jnp.float32
    )
    value = product[:PAIRS, :PAIRS] + product[PAIRS:, PAIRS:]
    width = PAIRS // devices
    for g in range(devices):
        parts[g] = value[g * width : (g + 1) * width]
    moves = []
    for k in range(1, devices):
        peer = (me + k) % devices
        copy = remote(
            parts.at[peer], arrived.at[k], sum_send.at[k], sum_recv.at[k], {"grid": peer}
        )
        copy.start()
        moves.append(copy)
    result = parts[me]
    for copy in moves:
        copy.wait()
    for copy in started:
        copy.wait_send()
    for k in range(1, devices):
        result = result + arrived[k]
    out_ref[...] = result


def tail(moved, mix, points, twin_points, screened, devices):
    vmem = pl.BlockSpec(memory_space=pltpu.VMEM)
    dma = pltpu.SemaphoreType.DMA
    width = PAIRS // devices
    side = (points.shape[1], 2 * PAIRS)
    both = (points.shape[1], 4 * PAIRS)
    table = (KF, 4 * PAIRS)
    return pl.pallas_call(
        functools.partial(tail_kernel, devices),
        out_shape=jax.ShapeDtypeStruct((width, PAIRS), jnp.float32),
        in_specs=[vmem] * 4 + [pl.BlockSpec(memory_space=pl.ANY)],
        out_specs=vmem,
        scratch_shapes=[
            pltpu.VMEM(both, jnp.bfloat16),
            pltpu.VMEM(both, jnp.bfloat16),
            pltpu.VMEM(table, jnp.bfloat16),
            pltpu.VMEM((NEG * ROWS_X, 4 * PAIRS), jnp.bfloat16),
            pltpu.VMEM(screened.shape, jnp.bfloat16),
            pltpu.VMEM(side, jnp.float32),
            pltpu.VMEM(both, jnp.bfloat16),
            pltpu.VMEM((devices // 2 - 1, *table), jnp.bfloat16),
            pltpu.VMEM(side, jnp.bfloat16),
            pltpu.VMEM(side, jnp.bfloat16),
            pltpu.VMEM((devices, *side), jnp.bfloat16),
            pltpu.VMEM((devices, width, PAIRS), jnp.float32),
            pltpu.VMEM((devices, width, PAIRS), jnp.float32),
            dma((1,)), dma((1,)), dma((1,)), dma((devices // 2 - 1,)),
            dma((devices,)), dma((devices,)), dma((1,)), dma((devices,)), dma((devices,)),
            dma((1,)),
        ],
        compiler_params=pltpu.CompilerParams(collective_id=1, has_side_effects=True),
        name="screen_and_sum",
    )(moved, mix, points, twin_points, screened)


def per_device(devices, valence, conduction, screened, blocks, gsphere):
    held_blocks = valence.shape[0] // BLK
    planes = conduction.shape[1]
    by_plane = jnp.transpose(valence, (1, 0, 2)).reshape(planes, held_blocks, BLK, LANES)
    chosen = spread(blocks, by_plane)
    points = gsphere[None]
    moved, twin_points = densities(
        chosen, jnp.transpose(conduction, (1, 0, 2)), jnp.asarray(z_matrix()),
        jnp.asarray(y_matrix()), points, devices,
    )
    return tail(moved, jnp.asarray(x_matrix()), points, twin_points, screened, devices)[None]


def solution(mesh):
    in_specs = (P("band", "grid", None), P("band", "grid", None), P("grid", None), P(), P("grid"))
    return jax.shard_map(
        functools.partial(per_device, mesh.shape["grid"]), mesh=mesh, in_specs=in_specs,
        out_specs=P("band", "grid", None), check_vma=False,
    )
```
